256 devices in a mesh: ctxa: 32 (over x, z), ctxb: 8 (over y, core).
Axes of the slice: x: 4, y: 4, z: 8, core: 2. Of those that a mesh axis runs over, the one named last changes fastest.
Arguments:
- tokens: bfloat16 [32768, 1024], P(('ctxa', 'ctxb')), may hold values from -80 to 80
- w_query: bfloat16 [1024, 512], replicated, may hold values from -0.1875 to 0.1875
- w_key: bfloat16 [1024, 512], replicated, may hold values from -0.1875 to 0.1875
- w_value: bfloat16 [1024, 512], replicated, may hold values from -0.1875 to 0.1875
- w_slot: bfloat16 [8, 64, 128], replicated, may hold values from -3 to 3
- w_out: bfloat16 [512, 1024], replicated, may hold values from -1 to 1
Outputs:
- mixed: bfloat16 [32768, 1024], P(('ctxa', 'ctxb'))
The draws below stay inside these ranges and needn't reach their ends.
All inputs are finite; a program needn't handle non-finite values.
Results may differ from the reference program's by a relative error of at most 0.012.
The reference program's roundings to bfloat16 on the way count: a program that leaves them out, or rounds other values in their place, can miss the bound.
Values may be sent and summed in bfloat16 or wider, within the bound.
A program may use at most 192 MiB of HBM per device.

```python
import jax
import jax.numpy as jnp
from jax import lax

D = 1024
HEADS = 8
HEAD_DIM = 64
SLOTS = 128
WINDOW = 128
TOK_DEV = 128
SEQ = 32768


def draw_tokens(key, part):
    keys = jax.random.split(jax.random.fold_in(key, 11), 1)
    base = jnp.clip(jax.random.normal(keys[0], (SEQ, D), jnp.float32), -6.0, 6.0)
    return base.astype(jnp.bfloat16)


def centred(rng, extent, scale, reach, held_as=jnp.bfloat16):
    drawn = scale * jax.random.normal(rng, extent, jnp.float32)
    return jnp.clip(drawn, min=-reach, max=reach).astype(held_as)


def setup_inputs(seed: int = 0) -> dict:
    splits = jax.random.split(jax.random.key(seed), 7)
    tokens = draw_tokens(jax.random.fold_in(splits[6], 71), 0)
    w_query = centred(splits[1], (D, HEADS * HEAD_DIM), D ** -0.5, 0.1875)
    w_key = centred(splits[2], (D, HEADS * HEAD_DIM), D ** -0.5, 0.1875)
    w_value = centred(splits[3], (D, HEADS * HEAD_DIM), D ** -0.5, 0.1875)
    w_slot = centred(splits[4], (HEADS, HEAD_DIM, SLOTS), 0.5, 3.0)
    w_out = centred(splits[5], (HEADS * HEAD_DIM, D), (HEADS * HEAD_DIM // 16) ** -0.5, 1.0)
    return {"tokens": tokens, "w_query": w_query, "w_key": w_key, "w_value": w_value, "w_slot": w_slot, "w_out": w_out}


def layer_norm(values):
    center = values - lax.optimization_barrier(jnp.mean(values, axis=-1, keepdims=True))
    spread = lax.optimization_barrier(jnp.mean(center * center, axis=-1, keepdims=True))
    return center * lax.rsqrt(spread + 1e-05)

def reference(tokens, w_query, w_key, w_value, w_slot, w_out):
    width = HEADS * HEAD_DIM
    query = jnp.dot(tokens, w_query, preferred_element_type=jnp.float32).astype(jnp.bfloat16)
    key = jnp.dot(tokens, w_key, preferred_element_type=jnp.float32).astype(jnp.bfloat16)
    value = jnp.dot(tokens, w_value, preferred_element_type=jnp.float32).astype(jnp.bfloat16)

    def slot_head(head):
        first = (head * HEAD_DIM).astype(jnp.int32)
        key_head = lax.dynamic_slice_in_dim(key, first, HEAD_DIM, 1).astype(jnp.float32)
        value_head = lax.dynamic_slice_in_dim(value, first, HEAD_DIM, 1).astype(jnp.float32)
        slot_map = lax.dynamic_index_in_dim(w_slot, head, 0, keepdims=False).astype(jnp.float32)
        logits = jnp.dot(key_head, slot_map, precision=lax.Precision.HIGHEST)
        top = lax.optimization_barrier(jnp.max(logits, axis=0))
        weight = jnp.exp(logits - top[None, :])
        total = lax.optimization_barrier(jnp.sum(weight, axis=0))
        paired = jnp.concatenate([key_head, value_head], axis=1)
        sums = jnp.dot(weight.T, paired, precision=lax.Precision.HIGHEST)
        slot_keys = layer_norm(sums[:, :HEAD_DIM])
        slot_values = sums[:, HEAD_DIM:] / total[:, None]
        return (slot_keys.astype(jnp.bfloat16), slot_values.astype(jnp.bfloat16))
    slot_keys, slot_values = lax.map(slot_head, jnp.arange(HEADS, dtype=jnp.int32))
    near_keys = layer_norm(key.reshape(SEQ, HEADS, HEAD_DIM).astype(jnp.float32)).astype(jnp.bfloat16)
    near_keys = near_keys.reshape(SEQ, width)
    padded_keys = jnp.pad(near_keys, ((WINDOW, WINDOW), (0, 0)))
    padded_values = jnp.pad(value, ((WINDOW, WINDOW), (0, 0)))
    block = min(512, TOK_DEV)
    span = block + 2 * WINDOW
    scale = 1.0 / HEAD_DIM ** 0.5

    def attend(index):
        start = (index * block).astype(jnp.int32)
        query_block = lax.dynamic_slice_in_dim(query, start, block, 0).reshape(block, HEADS, HEAD_DIM).astype(jnp.float32)
        keys_block = lax.dynamic_slice_in_dim(padded_keys, start, span, 0).reshape(span, HEADS, HEAD_DIM).astype(jnp.float32)
        values_block = lax.dynamic_slice_in_dim(padded_values, start, span, 0).reshape(span, HEADS, HEAD_DIM).astype(jnp.float32)
        query_pos = start + jnp.arange(block, dtype=jnp.int32)
        key_pos = start - WINDOW + jnp.arange(span, dtype=jnp.int32)
        valid = (jnp.abs(key_pos[None, :] - query_pos[:, None]) <= WINDOW) & (key_pos[None, :] >= 0) & (key_pos[None, :] < SEQ)
        near = jnp.einsum('bhd,khd->hbk', query_block, keys_block) * scale
        near = jnp.where(valid[None], near, -1e+30)
        far = jnp.einsum('bhd,hsd->hbs', query_block, slot_keys.astype(jnp.float32)) * scale
        top = jnp.maximum(lax.optimization_barrier(jnp.max(near, axis=-1)), lax.optimization_barrier(jnp.max(far, axis=-1)))
        near_exp = jnp.exp(near - top[..., None])
        far_exp = jnp.exp(far - top[..., None])
        denom = lax.optimization_barrier(jnp.sum(near_exp, axis=-1)) + lax.optimization_barrier(jnp.sum(far_exp, axis=-1))
        near_probs = (near_exp / denom[..., None]).astype(jnp.bfloat16).astype(jnp.float32)
        far_probs = (far_exp / denom[..., None]).astype(jnp.bfloat16).astype(jnp.float32)
        result = jnp.einsum('hbk,khd->bhd', near_probs, values_block)
        result = result + jnp.einsum('hbs,hsd->bhd', far_probs, slot_values.astype(jnp.float32))
        return result.reshape(block, width).astype(jnp.bfloat16)
    attended = lax.map(attend, jnp.arange(SEQ // block, dtype=jnp.int32)).reshape(SEQ, width)
    return jnp.dot(attended, w_out, preferred_element_type=jnp.float32).astype(jnp.bfloat16)
```

```python
import jax
import jax.numpy as jnp
from jax import lax
from jax.experimental import pallas as pl
from jax.experimental.pallas import tpu as pltpu
from jax.sharding import PartitionSpec as P

HEADS = 8
HEAD_DIM = 64
SLOTS = 128
WINDOW = 128
ROWS = 128
D = 1024
WIDTH = HEADS * HEAD_DIM

NX = 4
NZ = 8
NB = 8
PLANE = NX * NB
DEVICES = PLANE * NZ
UNIT = 32
MSG = 40
SLOT_ROWS = 48

BF16 = jnp.bfloat16
F32 = jnp.float32
MESH = pl.DeviceIdType.MESH
NT = (((1,), (1,)), ((), ()))
TN = (((0,), (0,)), ((), ()))


def dot(a, b):
    return jnp.dot(a, b, preferred_element_type=F32)


def stats_block(top, total):
    row = lax.broadcasted_iota(jnp.int32, (8, SLOTS), 0)
    both = jnp.where(row < 3, top, total)
    high = both.astype(BF16).astype(F32)
    rest = both - high
    mid = rest.astype(BF16).astype(F32)
    low = rest - mid
    part = jnp.where(row < 3, row, row - 3)
    return jnp.where(part == 0, high, jnp.where(part == 1, mid, jnp.where(part == 2, low, 0.0)))


def merge(load_stats, load_data, count):
    stats = [load_stats(k).astype(F32) for k in range(count)]
    tops = [s[0:1] + s[1:2] + s[2:3] for s in stats]
    totals = [s[3:4] + s[4:5] + s[5:6] for s in stats]
    top = tops[0]
    for other in tops[1:]:
        top = jnp.maximum(top, other)
    total = jnp.zeros_like(top)
    sums = jnp.zeros((UNIT, SLOTS), F32)
    for k in range(count):
        scale = jnp.exp(tops[k] - top)
        total = total + scale * totals[k]
        sums = sums + scale * load_data(k).astype(F32)
    return top, total, sums


def layer(
    tok_hbm,
    wq_hbm,
    wk_hbm,
    wv_hbm,
    ws_hbm,
    wo_hbm,
    out_ref,
    tok,
    wq,
    wk,
    wv,
    ws,
    wo,
    in_sem,
    block_diag,
    key_ref,
    key_t,
    query_t,
    units,
    rs_in,
    z_out,
    z_in,
    slots,
    near,
    acc,
    near_top,
    near_sum,
    rs_send,
    rs_recv,
    z_send,
    z_recv,
    ag_send,
    ag_recv,
    halo_send,
    halo_recv,
):
    a = lax.axis_index("ctxa")
    b = lax.axis_index("ctxb")
    x = lax.div(a, NZ)
    z = lax.rem(a, NZ)
    me = x * NB + b
    line = a * NB + b

    copies = [
        pltpu.make_async_copy(src, dst, in_sem.at[i])
        for i, (src, dst) in enumerate(
            ((tok_hbm, tok), (wk_hbm, wk), (wv_hbm, wv), (ws_hbm, ws), (wq_hbm, wq), (wo_hbm, wo))
        )
    ]
    for copy in copies:
        copy.start()

    def plane_id(dx, db):
        tx = lax.rem(x + dx, NX)
        tb = lax.rem(b + db, NB)
        return tx, tb, (tx * NZ + z, tb)

    def line_id(step):
        other = lax.rem(line + step, DEVICES)
        return (lax.div(other, NB), lax.rem(other, NB))

    barrier = pltpu.get_barrier_semaphore()

    def greet_plane(k, carry):
        _, _, device = plane_id(lax.div(k, NB), lax.rem(k, NB))
        pl.semaphore_signal(barrier, inc=1, device_id=device, device_id_type=MESH)
        return carry

    def greet_z(k, carry):
        pl.semaphore_signal(
            barrier, inc=1, device_id=(x * NZ + lax.rem(z + k, NZ), b), device_id_type=MESH
        )
        return carry

    lax.fori_loop(1, PLANE, greet_plane, 0)
    lax.fori_loop(1, NZ, greet_z, 0)
    for step in (1, DEVICES - 1):
        pl.semaphore_signal(barrier, inc=1, device_id=line_id(step), device_id_type=MESH)

    def rs_copy(dx, db):
        tx, tb, device = plane_id(dx, db)
        slot = dx * NB + db
        return pltpu.make_async_remote_copy(
            src_ref=units.at[tx * NB + tb, pl.ds(0, MSG)],
            dst_ref=rs_in.at[slot, pl.ds(0, MSG)],
            send_sem=rs_send.at[slot],
            recv_sem=rs_recv.at[slot],
            device_id=device,
            device_id_type=MESH,
        )

    def z_copy(dz):
        return pltpu.make_async_remote_copy(
            src_ref=z_out.at[pl.ds(0, MSG)],
            dst_ref=z_in.at[dz, pl.ds(0, MSG)],
            send_sem=z_send.at[dz],
            recv_sem=z_recv.at[dz],
            device_id=(x * NZ + lax.rem(z + dz, NZ), b),
            device_id_type=MESH,
        )

    def ag_copy(dx, db):
        _, _, device = plane_id(dx, db)
        slot = dx * NB + db
        return pltpu.make_async_remote_copy(
            src_ref=slots.at[me],
            dst_ref=slots.at[me],
            send_sem=ag_send.at[slot],
            recv_sem=ag_recv.at[slot],
            device_id=device,
            device_id_type=MESH,
        )

    def halo_copy(side):
        return pltpu.make_async_remote_copy(
            src_ref=near.at[1],
            dst_ref=near.at[2 * side],
            send_sem=halo_send.at[side],
            recv_sem=halo_recv.at[side],
            device_id=line_id(1 if side == 0 else DEVICES - 1),
            device_id_type=MESH,
        )

    copies[0].wait()
    copies[1].wait()
    key = dot(tok[...], wk[...]).astype(BF16)
    key_ref[...] = key
    key_t[...] = key.T
    copies[2].wait()
    value_t = dot(tok[...], wv[...]).astype(BF16).T
    near[1, WIDTH:, :] = value_t
    copies[3].wait()
    zero = jnp.zeros((HEAD_DIM, SLOTS), BF16)
    for pair in range(HEADS // 2):
        block_diag[pair, 0:HEAD_DIM, 0:SLOTS] = ws[2 * pair]
        block_diag[pair, 0:HEAD_DIM, SLOTS:] = zero
        block_diag[pair, HEAD_DIM:, 0:SLOTS] = zero
        block_diag[pair, HEAD_DIM:, SLOTS:] = ws[2 * pair + 1]

    db_order = (4, 3, 5, 2, 6, 1, 7, 0)
    for step, dx in enumerate((2, 1, 3, 0)):
        pair = lax.rem(x + dx, NX)
        columns = pl.ds(pl.multiple_of(pair * 2 * HEAD_DIM, 2 * HEAD_DIM), 2 * HEAD_DIM)
        logits = dot(key_ref[:, columns], block_diag[pair])
        top = jnp.max(logits, axis=0, keepdims=True)
        weight = jnp.exp(logits - top)
        total = jnp.sum(weight, axis=0, keepdims=True)
        weight_high = weight.astype(BF16)
        weight_low = (weight - weight_high.astype(F32)).astype(BF16)
        for head in range(2):
            cols = slice(head * SLOTS, (head + 1) * SLOTS)
            high, low = weight_high[:, cols], weight_low[:, cols]
            first = pl.multiple_of(pair * 2 * HEAD_DIM + head * HEAD_DIM, HEAD_DIM)
            keys_h = key_t[pl.ds(first, HEAD_DIM), :]
            values_h = near[1, pl.ds(WIDTH + first, HEAD_DIM), :]
            key_sum = dot(keys_h, high) + dot(keys_h, low)
            key_sum = key_sum - jnp.mean(key_sum, axis=0, keepdims=True)
            value_sum = dot(values_h, high) + dot(values_h, low)
            stats = stats_block(top[:, cols], total[:, cols]).astype(BF16)
            for quarter, data in enumerate(
                (key_sum[:UNIT], key_sum[UNIT:], value_sum[:UNIT], value_sum[UNIT:])
            ):
                unit = pair * NB + head * 4 + quarter
                units[unit, 0:UNIT, :] = data.astype(BF16)
                units[unit, UNIT:MSG, :] = stats
        if step == 0:
            pl.semaphore_wait(barrier, PLANE + NZ)
        for db in db_order:
            if dx or db:
                rs_copy(dx, db).start()

    for head in range(HEADS):
        rows = slice(head * HEAD_DIM, (head + 1) * HEAD_DIM)
        values = key_t[rows, :].astype(F32)
        center = values - jnp.mean(values, axis=0, keepdims=True)
        spread = jnp.mean(center * center, axis=0, keepdims=True)
        near[1, rows, :] = (center * lax.rsqrt(spread + 1e-05)).astype(BF16)
    copies[4].wait()
    query = dot(tok[...], wq[...]).astype(BF16).astype(F32) * (1.0 / HEAD_DIM**0.5)
    query_t[...] = query.astype(BF16).T

    for slot in range(1, PLANE):
        rs_copy(slot // NB, slot % NB).wait_recv()

    rs_in[0, 0:MSG] = units[me, 0:MSG]
    top, total, sums = merge(
        lambda k: rs_in[k, UNIT:MSG, :], lambda k: rs_in[k, 0:UNIT, :], PLANE
    )
    z_out[0:UNIT, :] = sums.astype(BF16)
    z_out[UNIT:MSG, :] = stats_block(top, total).astype(BF16)
    for dz in (4, 3, 5, 2, 6, 1, 7):
        z_copy(dz).start()
    for side in range(2):
        halo_copy(side).start()
    for dz in range(1, NZ):
        z_copy(dz).wait_recv()
    z_in[0, 0:MSG] = z_out[0:MSG]
    top, total, sums = merge(lambda k: z_in[k, UNIT:MSG, :], lambda k: z_in[k, 0:UNIT, :], NZ)
    is_value = lax.rem(me, 4) >= 2
    divisor = jnp.where(is_value, total, 1.0)
    slots[me] = (sums / divisor).astype(BF16)
    for dx in (2, 1, 3, 0):
        for db in db_order:
            if dx or db:
                ag_copy(dx, db).start()

    for side in range(2):
        halo_copy(side).wait_recv()
    source = lax.broadcasted_iota(jnp.int32, (ROWS, ROWS), 0)
    target = lax.broadcasted_iota(jnp.int32, (ROWS, ROWS), 1)
    before = (source >= target) & (line > 0)
    after = (source <= target) & (line < DEVICES - 1)
    for head in range(HEADS):
        rows = slice(head * HEAD_DIM, (head + 1) * HEAD_DIM)
        value_rows = slice(WIDTH + head * HEAD_DIM, WIDTH + (head + 1) * HEAD_DIM)
        query_h = query_t[rows, :]
        scores = [
            lax.dot_general(near[i, rows, :], query_h, TN, preferred_element_type=F32)
            for i in range(3)
        ]
        scores[0] = jnp.where(before, scores[0], -1e30)
        scores[2] = jnp.where(after, scores[2], -1e30)
        top_h = jnp.max(
            jnp.maximum(jnp.maximum(scores[0], scores[1]), scores[2]), axis=0, keepdims=True
        )
        exps = [jnp.exp(s - top_h) for s in scores]
        near_top[head : head + 1, :] = top_h
        near_sum[head : head + 1, :] = jnp.sum(exps[0] + exps[1] + exps[2], axis=0, keepdims=True)
        total_h = dot(near[0, value_rows, :], exps[0].astype(BF16))
        total_h = total_h + dot(near[1, value_rows, :], exps[1].astype(BF16))
        acc[rows, :] = total_h + dot(near[2, value_rows, :], exps[2].astype(BF16))

    for slot in range(1, PLANE):
        ag_copy(slot // NB, slot % NB).wait_recv()

    copies[5].wait()
    attended = []
    for head in range(HEADS):
        rows = slice(head * HEAD_DIM, (head + 1) * HEAD_DIM)
        center = slots[4 * head : 4 * head + 2].reshape(HEAD_DIM, SLOTS).astype(F32)
        values_h = slots[4 * head + 2 : 4 * head + 4].reshape(HEAD_DIM, SLOTS)
        spread = jnp.mean(center * center, axis=0, keepdims=True)
        keys_h = (center * lax.rsqrt(spread + 1e-05)).astype(BF16)
        scores = lax.dot_general(keys_h, query_t[rows, :], TN, preferred_element_type=F32)
        top_n = near_top[head : head + 1, :]
        top_h = jnp.maximum(top_n, jnp.max(scores, axis=0, keepdims=True))
        exps = jnp.exp(scores - top_h)
        scale = jnp.exp(top_n - top_h)
        denom = scale * near_sum[head : head + 1, :] + jnp.sum(exps, axis=0, keepdims=True)
        result = scale * acc[rows, :] + dot(values_h, exps.astype(BF16))
        attended.append((result / denom).astype(BF16))
    attended = jnp.concatenate(attended, axis=0)
    out_ref[...] = lax.dot_general(
        attended, wo[...], TN, preferred_element_type=F32
    ).astype(BF16)

    for slot in range(1, PLANE):
        rs_copy(slot // NB, slot % NB).wait_send()
        ag_copy(slot // NB, slot % NB).wait_send()
    for dz in range(1, NZ):
        z_copy(dz).wait_send()
    for side in range(2):
        halo_copy(side).wait_send()


def per_device(tokens, w_query, w_key, w_value, w_slot, w_out):
    dma = pltpu.SemaphoreType.DMA
    return pl.pallas_call(
        layer,
        out_shape=jax.ShapeDtypeStruct((ROWS, D), BF16),
        in_specs=[pl.BlockSpec(memory_space=pl.ANY)] * 6,
        out_specs=pl.BlockSpec(memory_space=pltpu.VMEM),
        scratch_shapes=[
            pltpu.VMEM((ROWS, D), BF16),
            pltpu.VMEM((D, WIDTH), BF16),
            pltpu.VMEM((D, WIDTH), BF16),
            pltpu.VMEM((D, WIDTH), BF16),
            pltpu.VMEM((HEADS, HEAD_DIM, SLOTS), BF16),
            pltpu.VMEM((WIDTH, D), BF16),
            dma((6,)),
            pltpu.VMEM((HEADS // 2, 2 * HEAD_DIM, 2 * SLOTS), BF16),
            pltpu.VMEM((ROWS, WIDTH), BF16),
            pltpu.VMEM((WIDTH, ROWS), BF16),
            pltpu.VMEM((WIDTH, ROWS), BF16),
            pltpu.VMEM((PLANE, SLOT_ROWS, SLOTS), BF16),
            pltpu.VMEM((PLANE, SLOT_ROWS, SLOTS), BF16),
            pltpu.VMEM((SLOT_ROWS, SLOTS), BF16),
            pltpu.VMEM((NZ, SLOT_ROWS, SLOTS), BF16),
            pltpu.VMEM((PLANE, UNIT, SLOTS), BF16),
            pltpu.VMEM((3, 2 * WIDTH, ROWS), BF16),
            pltpu.VMEM((WIDTH, ROWS), F32),
            pltpu.VMEM((HEADS, ROWS), F32),
            pltpu.VMEM((HEADS, ROWS), F32),
            dma((PLANE,)),
            dma((PLANE,)),
            dma((NZ,)),
            dma((NZ,)),
            dma((PLANE,)),
            dma((PLANE,)),
            dma((2,)),
            dma((2,)),
        ],
        compiler_params=pltpu.CompilerParams(collective_id=0, has_side_effects=True),
        name="layer",
    )(tokens, w_query, w_key, w_value, w_slot, w_out)


def solution(mesh):
    in_specs = (P(("ctxa", "ctxb"), None), P(), P(), P(), P(), P())
    out_specs = P(("ctxa", "ctxb"), None)
    return jax.shard_map(
        per_device, mesh=mesh, in_specs=in_specs, out_specs=out_specs, check_vma=False
    )
```

```python
import jax
import jax.numpy as jnp
from jax import lax
from jax.experimental import pallas as pl
from jax.experimental.pallas import tpu as pltpu
from jax.sharding import PartitionSpec as P

HEADS = 8
HEAD_DIM = 64
SLOTS = 128
WINDOW = 128
ROWS = 128
D = 1024
WIDTH = HEADS * HEAD_DIM

NX = 4
NZ = 8
NB = 8
PLANE = NX * NB
DEVICES = PLANE * NZ
UNIT = 32
MSG = 40
SLOT_ROWS = 48

BF16 = jnp.bfloat16
F32 = jnp.float32
MESH = pl.DeviceIdType.MESH
TN = (((0,), (0,)), ((), ()))


def dot(a, b):
    return jnp.dot(a, b, preferred_element_type=F32)


def stats_block(top, total):
    row = lax.broadcasted_iota(jnp.int32, (8, SLOTS), 0)
    both = jnp.where(row < 3, top, total)
    high = both.astype(BF16).astype(F32)
    rest = both - high
    mid = rest.astype(BF16).astype(F32)
    low = rest - mid
    part = jnp.where(row < 3, row, row - 3)
    return jnp.where(part == 0, high, jnp.where(part == 1, mid, jnp.where(part == 2, low, 0.0)))


def merge(parts, running=None):
    stats = [load_stats().astype(F32) for load_stats, _ in parts]
    tops = [s[0:1] + s[1:2] + s[2:3] for s in stats]
    totals = [s[3:4] + s[4:5] + s[5:6] for s in stats]
    top = tops[0]
    for other in tops[1:]:
        top = jnp.maximum(top, other)
    if running is None:
        total = jnp.zeros_like(top)
        sums = jnp.zeros((UNIT, SLOTS), F32)
    else:
        old_top, total, sums = running
        top = jnp.maximum(top, old_top)
        scale = jnp.exp(old_top - top)
        total, sums = scale * total, scale * sums
    for k, (_, load_data) in enumerate(parts):
        scale = jnp.exp(tops[k] - top)
        total = total + scale * totals[k]
        sums = sums + scale * load_data().astype(F32)
    return top, total, sums


def layer(
    tok_hbm,
    wq_hbm,
    wk_hbm,
    wv_hbm,
    ws_hbm,
    out_ref,
    tok,
    wq,
    wk,
    wv,
    ws,
    in_sem,
    block_diag,
    key_ref,
    key_t,
    query_t,
    units,
    rs_in,
    z_out,
    z_in,
    slots,
    near,
    relay,
    acc,
    near_top,
    near_sum,
    rs_send,
    rs_recv,
    z_send,
    z_recv,
    ag_send,
    ag_recv,
    halo_send,
    halo_recv,
    relay_send,
    relay_recv,
):
    a = lax.axis_index("ctxa")
    b = lax.axis_index("ctxb")
    x = a >> 3
    z = a & (NZ - 1)
    me = x * NB + b

    pairs = ((ws_hbm, ws), (tok_hbm, tok), (wk_hbm, wk), (wv_hbm, wv), (wq_hbm, wq))
    copies = [
        pltpu.make_async_copy(src, dst, in_sem.at[i]) for i, (src, dst) in enumerate(pairs)
    ]
    for copy in copies[:4]:
        copy.start()

    def device(dx=0, dz=0, db=0):
        return ((((x + dx) & (NX - 1)) << 3) | ((z + dz) & (NZ - 1)), (b + db) & (NB - 1))

    db_order = (4, 3, 5, 2, 6, 1, 7, 0)
    dz_order = (4, 3, 5, 2, 6, 1, 7)
    barrier = pltpu.get_barrier_semaphore()
    for dx in (2, 1, 3, 0):
        for db in db_order:
            if dx or db:
                pl.semaphore_signal(
                    barrier, inc=1, device_id=device(dx=dx, db=db), device_id_type=MESH
                )
    for dz in dz_order:
        pl.semaphore_signal(barrier, inc=1, device_id=device(dz=dz), device_id_type=MESH)

    def rs_copy(dx, db):
        unit = (((x + dx) & (NX - 1)) << 3) | ((b + db) & (NB - 1))
        return pltpu.make_async_remote_copy(
            src_ref=units.at[unit, pl.ds(0, MSG)],
            dst_ref=rs_in.at[dx * NB + db, pl.ds(0, MSG)],
            send_sem=rs_send.at[0],
            recv_sem=rs_recv.at[dx],
            device_id=device(dx=dx, db=db),
            device_id_type=MESH,
        )

    def z_copy(dz):
        return pltpu.make_async_remote_copy(
            src_ref=z_out.at[pl.ds(0, MSG)],
            dst_ref=z_in.at[dz, pl.ds(0, MSG)],
            send_sem=z_send.at[0],
            recv_sem=z_recv.at[0],
            device_id=device(dz=dz),
            device_id_type=MESH,
        )

    def ag_copy(dx, db):
        return pltpu.make_async_remote_copy(
            src_ref=slots.at[me],
            dst_ref=slots.at[me],
            send_sem=ag_send.at[0],
            recv_sem=ag_recv.at[dx],
            device_id=device(dx=dx, db=db),
            device_id_type=MESH,
        )

    def halo_copy(side, src, target):
        return pltpu.make_async_remote_copy(
            src_ref=src,
            dst_ref=near.at[2 * side],
            send_sem=halo_send.at[side],
            recv_sem=halo_recv.at[side],
            device_id=target,
            device_id_type=MESH,
        )

    def relay_copy(side):
        return pltpu.make_async_remote_copy(
            src_ref=near.at[1],
            dst_ref=relay,
            send_sem=relay_send.at[0],
            recv_sem=relay_recv.at[0],
            device_id=device(dz=1 if side == 0 else NZ - 1),
            device_id_type=MESH,
        )

    last, first = b == NB - 1, b == 0
    halo_next = halo_copy(0, near.at[1], device(db=1))
    halo_prev = halo_copy(1, near.at[1], device(db=NB - 1))
    cross_next = halo_copy(0, relay, device(dx=jnp.where(z == 0, 1, 0), db=1))
    cross_prev = halo_copy(1, relay, device(dx=jnp.where(z == NZ - 1, NX - 1, 0), db=NB - 1))

    def group_wait(ref, sem):
        pltpu.make_async_copy(ref, ref, sem).wait()

    copies[0].wait()
    zero = jnp.zeros((HEAD_DIM, SLOTS), BF16)
    for pair in range(HEADS // 2):
        block_diag[pair, 0:HEAD_DIM, 0:SLOTS] = ws[2 * pair]
        block_diag[pair, 0:HEAD_DIM, SLOTS:] = zero
        block_diag[pair, HEAD_DIM:, 0:SLOTS] = zero
        block_diag[pair, HEAD_DIM:, SLOTS:] = ws[2 * pair + 1]
    copies[1].wait()
    copies[2].wait()
    key = dot(tok[...], wk[...]).astype(BF16)
    copies[4].start()
    key_ref[...] = key
    key_t[...] = key.T
    copies[3].wait()
    near[1, WIDTH:, :] = dot(tok[...], wv[...]).astype(BF16).T

    for step, dx in enumerate((2, 1, 3, 0)):
        pair = (x + dx) & (NX - 1)
        columns = pl.ds(pl.multiple_of(pair * 2 * HEAD_DIM, 2 * HEAD_DIM), 2 * HEAD_DIM)
        logits = dot(key_ref[:, columns], block_diag[pair])
        top = jnp.max(logits, axis=0, keepdims=True)
        weight = jnp.exp(logits - top)
        total = jnp.sum(weight, axis=0, keepdims=True)
        weight_high = weight.astype(BF16)
        weight_low = (weight - weight_high.astype(F32)).astype(BF16)
        for head in range(2):
            cols = slice(head * SLOTS, (head + 1) * SLOTS)
            high, low = weight_high[:, cols], weight_low[:, cols]
            start = pl.multiple_of(pair * 2 * HEAD_DIM + head * HEAD_DIM, HEAD_DIM)
            keys_h = key_t[pl.ds(start, HEAD_DIM), :]
            values_h = near[1, pl.ds(WIDTH + start, HEAD_DIM), :]
            key_sum = dot(keys_h, high) + dot(keys_h, low)
            key_sum = key_sum - jnp.mean(key_sum, axis=0, keepdims=True)
            value_sum = dot(values_h, high) + dot(values_h, low)
            stats = stats_block(top[:, cols], total[:, cols]).astype(BF16)
            for quarter, data in enumerate(
                (key_sum[:UNIT], key_sum[UNIT:], value_sum[:UNIT], value_sum[UNIT:])
            ):
                unit = pair * NB + head * 4 + quarter
                units[unit, 0:UNIT, :] = data.astype(BF16)
                units[unit, UNIT:MSG, :] = stats
        if step == 0:
            pl.semaphore_wait(barrier, PLANE + NZ - 2)
        for db in db_order:
            if dx or db:
                rs_copy(dx, db).start()

    for head in range(HEADS):
        rows = slice(head * HEAD_DIM, (head + 1) * HEAD_DIM)
        values = key_t[rows, :].astype(F32)
        center = values - jnp.mean(values, axis=0, keepdims=True)
        spread = jnp.mean(center * center, axis=0, keepdims=True)
        near[1, rows, :] = (center * lax.rsqrt(spread + 1e-05)).astype(BF16)
    pl.when(last)(lambda: relay_copy(0).start())
    pl.when(first)(lambda: relay_copy(1).start())
    copies[4].wait()
    query = dot(tok[...], wq[...]).astype(BF16).astype(F32) * (1.0 / HEAD_DIM**0.5)
    query_t[...] = query.astype(BF16).T

    running = None
    for dx in (0, 1, 3, 2):
        low = 1 if dx == 0 else 0
        group_wait(rs_in.at[pl.ds(dx * NB + low, NB - low), pl.ds(0, MSG)], rs_recv.at[dx])
        parts = [
            (lambda k=k: rs_in[k, UNIT:MSG, :], lambda k=k: rs_in[k, 0:UNIT, :])
            for k in range(dx * NB + low, (dx + 1) * NB)
        ]
        if dx == 0:
            parts.append((lambda: units[me, UNIT:MSG, :], lambda: units[me, 0:UNIT, :]))
        running = merge(parts, running)
    top, total, sums = running
    z_out[0:UNIT, :] = sums.astype(BF16)
    z_out[UNIT:MSG, :] = stats_block(top, total).astype(BF16)
    for dz in dz_order:
        z_copy(dz).start()

    @pl.when(last)
    def _():
        relay_copy(0).wait_recv()
        cross_next.start()

    @pl.when(first)
    def _():
        relay_copy(1).wait_recv()
        cross_prev.start()

    pl.when(jnp.logical_not(last))(halo_next.start)
    pl.when(jnp.logical_not(first))(halo_prev.start)
    group_wait(z_in.at[pl.ds(1, NZ - 1), pl.ds(0, MSG)], z_recv.at[0])
    parts = [
        (lambda k=k: z_in[k, UNIT:MSG, :], lambda k=k: z_in[k, 0:UNIT, :]) for k in range(1, NZ)
    ]
    parts.append((lambda: z_out[UNIT:MSG, :], lambda: z_out[0:UNIT, :]))
    top, total, sums = merge(parts)
    divisor = jnp.where((b & 3) >= 2, total, 1.0)
    slots[me] = (sums / divisor).astype(BF16)
    for dx in (2, 1, 3, 0):
        for db in db_order:
            if dx or db:
                ag_copy(dx, db).start()

    halo_next.wait_recv()
    halo_prev.wait_recv()
    source = lax.broadcasted_iota(jnp.int32, (ROWS, ROWS), 0)
    target = lax.broadcasted_iota(jnp.int32, (ROWS, ROWS), 1)
    line = a * NB + b
    before = (source >= target) & (line > 0)
    after = (source <= target) & (line < DEVICES - 1)
    for head in range(HEADS):
        rows = slice(head * HEAD_DIM, (head + 1) * HEAD_DIM)
        value_rows = slice(WIDTH + head * HEAD_DIM, WIDTH + (head + 1) * HEAD_DIM)
        query_h = query_t[rows, :]
        scores = [
            lax.dot_general(near[i, rows, :], query_h, TN, preferred_element_type=F32)
            for i in range(3)
        ]
        scores[0] = jnp.where(before, scores[0], -1e30)
        scores[2] = jnp.where(after, scores[2], -1e30)
        top_h = jnp.max(
            jnp.maximum(jnp.maximum(scores[0], scores[1]), scores[2]), axis=0, keepdims=True
        )
        exps = [jnp.exp(s - top_h) for s in scores]
        near_top[head] = jnp.broadcast_to(top_h, (8, ROWS))
        near_sum[head] = jnp.broadcast_to(
            jnp.sum(exps[0] + exps[1] + exps[2], axis=0, keepdims=True), (8, ROWS)
        )
        total_h = dot(near[0, value_rows, :], exps[0].astype(BF16))
        total_h = total_h + dot(near[1, value_rows, :], exps[1].astype(BF16))
        acc[rows, :] = total_h + dot(near[2, value_rows, :], exps[2].astype(BF16))

    for dx in (0, 1, 3, 2):
        low = 1 if dx == 0 else 0
        group_wait(slots.at[pl.ds(0, NB - low)], ag_recv.at[dx])
        pair = (x + NX - dx) & (NX - 1)
        results = []
        for half in range(2):
            head = pair * 2 + half
            start = pl.multiple_of(head * HEAD_DIM, HEAD_DIM)
            center = slots[pl.ds(4 * head, 2)].reshape(HEAD_DIM, SLOTS).astype(F32)
            values_h = slots[pl.ds(4 * head + 2, 2)].reshape(HEAD_DIM, SLOTS)
            spread = jnp.mean(center * center, axis=0, keepdims=True)
            keys_h = (center * lax.rsqrt(spread + 1e-05)).astype(BF16)
            scores = lax.dot_general(
                keys_h, query_t[pl.ds(start, HEAD_DIM), :], TN, preferred_element_type=F32
            )
            top_n = near_top[head, 0:1, :]
            top_h = jnp.maximum(top_n, jnp.max(scores, axis=0, keepdims=True))
            exps = jnp.exp(scores - top_h)
            scale = jnp.exp(top_n - top_h)
            denom = scale * near_sum[head, 0:1, :] + jnp.sum(exps, axis=0, keepdims=True)
            result = scale * acc[pl.ds(start, HEAD_DIM), :] + dot(values_h, exps.astype(BF16))
            results.append((result / denom).astype(BF16))
        columns = pl.ds(pl.multiple_of(pair * 2 * HEAD_DIM, 2 * HEAD_DIM), 2 * HEAD_DIM)
        out_ref[:, columns] = jnp.concatenate(results, axis=0).T

    group_wait(rs_in.at[pl.ds(0, PLANE - 1), pl.ds(0, MSG)], rs_send.at[0])
    group_wait(z_in.at[pl.ds(0, NZ - 1), pl.ds(0, MSG)], z_send.at[0])
    group_wait(slots.at[pl.ds(0, PLANE - 1)], ag_send.at[0])
    halo_next.wait_send()
    halo_prev.wait_send()
    pl.when(last | first)(relay_copy(0).wait_send)


def per_device(tokens, w_query, w_key, w_value, w_slot, w_out):
    dma = pltpu.SemaphoreType.DMA
    attended = pl.pallas_call(
        layer,
        out_shape=jax.ShapeDtypeStruct((ROWS, WIDTH), BF16),
        in_specs=[pl.BlockSpec(memory_space=pltpu.HBM)] * 5,
        out_specs=pl.BlockSpec(memory_space=pltpu.VMEM),
        scratch_shapes=[
            pltpu.VMEM((ROWS, D), BF16),
            pltpu.VMEM((D, WIDTH), BF16),
            pltpu.VMEM((D, WIDTH), BF16),
            pltpu.VMEM((D, WIDTH), BF16),
            pltpu.VMEM((HEADS, HEAD_DIM, SLOTS), BF16),
            dma((5,)),
            pltpu.VMEM((HEADS // 2, 2 * HEAD_DIM, 2 * SLOTS), BF16),
            pltpu.VMEM((ROWS, WIDTH), BF16),
            pltpu.VMEM((WIDTH, ROWS), BF16),
            pltpu.VMEM((WIDTH, ROWS), BF16),
            pltpu.VMEM((PLANE, SLOT_ROWS, SLOTS), BF16),
            pltpu.VMEM((PLANE, SLOT_ROWS, SLOTS), BF16),
            pltpu.VMEM((SLOT_ROWS, SLOTS), BF16),
            pltpu.VMEM((NZ, SLOT_ROWS, SLOTS), BF16),
            pltpu.VMEM((PLANE, UNIT, SLOTS), BF16),
            pltpu.VMEM((3, 2 * WIDTH, ROWS), BF16),
            pltpu.VMEM((2 * WIDTH, ROWS), BF16),
            pltpu.VMEM((WIDTH, ROWS), F32),
            pltpu.VMEM((HEADS, 8, ROWS), F32),
            pltpu.VMEM((HEADS, 8, ROWS), F32),
            dma((1,)),
            dma((NX,)),
            dma((1,)),
            dma((1,)),
            dma((1,)),
            dma((NX,)),
            dma((2,)),
            dma((2,)),
            dma((1,)),
            dma((1,)),
        ],
        compiler_params=pltpu.CompilerParams(
            collective_id=0, has_side_effects=True, vmem_limit_bytes=24 * 1024 * 1024
        ),
        name="layer",
    )(*(pltpu.with_memory_space_constraint(v, pltpu.HBM) for v in (tokens, w_query, w_key, w_value, w_slot)))
    return jnp.dot(attended, w_out, preferred_element_type=F32).astype(BF16)


def solution(mesh):
    in_specs = (P(("ctxa", "ctxb"), None), P(), P(), P(), P(), P())
    out_specs = P(("ctxa", "ctxb"), None)
    return jax.shard_map(
        per_device, mesh=mesh, in_specs=in_specs, out_specs=out_specs, check_vma=False
    )
```

```python
import jax
import jax.numpy as jnp
from jax import lax
from jax.experimental import pallas as pl
from jax.experimental.pallas import tpu as pltpu
from jax.sharding import PartitionSpec as P

HEADS = 8
HEAD_DIM = 64
SLOTS = 128
WINDOW = 128
ROWS = 128
D = 1024
WIDTH = HEADS * HEAD_DIM

NX = 4
NZ = 8
NB = 8
PLANE = NX * NB
DEVICES = PLANE * NZ
UNIT = 32
MSG = 40
SLOT_ROWS = 48

BF16 = jnp.bfloat16
F32 = jnp.float32
MESH = pl.DeviceIdType.MESH
TN = (((0,), (0,)), ((), ()))


def dot(a, b):
    return jnp.dot(a, b, preferred_element_type=F32)


def stats_block(top, total):
    row = lax.broadcasted_iota(jnp.int32, (8, SLOTS), 0)
    both = jnp.where(row < 3, top, total)
    high = both.astype(BF16).astype(F32)
    rest = both - high
    mid = rest.astype(BF16).astype(F32)
    low = rest - mid
    part = jnp.where(row < 3, row, row - 3)
    return jnp.where(part == 0, high, jnp.where(part == 1, mid, jnp.where(part == 2, low, 0.0)))


def merge(parts, running=None):
    stats = [load_stats().astype(F32) for load_stats, _ in parts]
    tops = [s[0:1] + s[1:2] + s[2:3] for s in stats]
    totals = [s[3:4] + s[4:5] + s[5:6] for s in stats]
    top = tops[0]
    for other in tops[1:]:
        top = jnp.maximum(top, other)
    if running is None:
        total = jnp.zeros_like(top)
        sums = jnp.zeros((UNIT, SLOTS), F32)
    else:
        old_top, total, sums = running
        top = jnp.maximum(top, old_top)
        scale = jnp.exp(old_top - top)
        total, sums = scale * total, scale * sums
    for k, (_, load_data) in enumerate(parts):
        scale = jnp.exp(tops[k] - top)
        total = total + scale * totals[k]
        sums = sums + scale * load_data().astype(F32)
    return top, total, sums


def layer(
    tok_hbm,
    wq_hbm,
    wk_hbm,
    wv_hbm,
    ws_hbm,
    out_ref,
    tok,
    wq,
    wk,
    wv,
    ws,
    in_sem,
    block_diag,
    key_ref,
    key_t,
    query_t,
    units,
    rs_in,
    z_out,
    z_in,
    slots,
    near,
    relay,
    acc,
    near_top,
    near_sum,
    rs_send,
    rs_recv,
    z_send,
    z_recv,
    ag_send,
    ag_recv,
    halo_send,
    halo_recv,
    relay_send,
    relay_recv,
):
    a = lax.axis_index("ctxa")
    b = lax.axis_index("ctxb")
    x = a >> 3
    z = a & (NZ - 1)
    me = x * NB + b

    pairs = ((ws_hbm, ws), (tok_hbm, tok), (wk_hbm, wk), (wv_hbm, wv), (wq_hbm, wq))
    copies = [
        pltpu.make_async_copy(src, dst, in_sem.at[i]) for i, (src, dst) in enumerate(pairs)
    ]
    for copy in copies[:4]:
        copy.start()

    def device(dx=0, dz=0, db=0):
        return ((((x + dx) & (NX - 1)) << 3) | ((z + dz) & (NZ - 1)), (b + db) & (NB - 1))

    db_order = (4, 3, 5, 2, 6, 1, 7, 0)
    dz_order = (4, 3, 5, 2, 6, 1, 7)
    barrier = pltpu.get_barrier_semaphore()
    for dx in (2, 1, 3, 0):
        for db in db_order:
            if dx or db:
                pl.semaphore_signal(
                    barrier, inc=1, device_id=device(dx=dx, db=db), device_id_type=MESH
                )
    for dz in dz_order:
        pl.semaphore_signal(barrier, inc=1, device_id=device(dz=dz), device_id_type=MESH)

    def rs_copy(dx, db):
        unit = (((x + dx) & (NX - 1)) << 3) | ((b + db) & (NB - 1))
        return pltpu.make_async_remote_copy(
            src_ref=units.at[unit, pl.ds(0, MSG)],
            dst_ref=rs_in.at[dx * NB + db, pl.ds(0, MSG)],
            send_sem=rs_send.at[0],
            recv_sem=rs_recv.at[dx],
            device_id=device(dx=dx, db=db),
            device_id_type=MESH,
        )

    def z_copy(dz):
        return pltpu.make_async_remote_copy(
            src_ref=z_out.at[pl.ds(0, MSG)],
            dst_ref=z_in.at[dz, pl.ds(0, MSG)],
            send_sem=z_send.at[0],
            recv_sem=z_recv.at[0],
            device_id=device(dz=dz),
            device_id_type=MESH,
        )

    def ag_copy(dx, db):
        return pltpu.make_async_remote_copy(
            src_ref=slots.at[me],
            dst_ref=slots.at[me],
            send_sem=ag_send.at[0],
            recv_sem=ag_recv.at[dx],
            device_id=device(dx=dx, db=db),
            device_id_type=MESH,
        )

    def halo_copy(side, src, target):
        return pltpu.make_async_remote_copy(
            src_ref=src,
            dst_ref=near.at[2 * side],
            send_sem=halo_send.at[side],
            recv_sem=halo_recv.at[side],
            device_id=target,
            device_id_type=MESH,
        )

    def relay_copy(side):
        return pltpu.make_async_remote_copy(
            src_ref=near.at[1],
            dst_ref=relay,
            send_sem=relay_send.at[0],
            recv_sem=relay_recv.at[0],
            device_id=device(dz=1 if side == 0 else NZ - 1),
            device_id_type=MESH,
        )

    last, first = b == NB - 1, b == 0
    halo_next = halo_copy(0, near.at[1], device(db=1))
    halo_prev = halo_copy(1, near.at[1], device(db=NB - 1))
    cross_next = halo_copy(0, relay, device(dx=jnp.where(z == 0, 1, 0), db=1))
    cross_prev = halo_copy(1, relay, device(dx=jnp.where(z == NZ - 1, NX - 1, 0), db=NB - 1))

    def group_wait(ref, sem):
        pltpu.make_async_copy(ref, ref, sem).wait()

    copies[0].wait()
    zero = jnp.zeros((HEAD_DIM, SLOTS), BF16)
    for pair in range(HEADS // 2):
        block_diag[pair, 0:HEAD_DIM, 0:SLOTS] = ws[2 * pair]
        block_diag[pair, 0:HEAD_DIM, SLOTS:] = zero
        block_diag[pair, HEAD_DIM:, 0:SLOTS] = zero
        block_diag[pair, HEAD_DIM:, SLOTS:] = ws[2 * pair + 1]
    copies[1].wait()
    copies[2].wait()
    key = dot(tok[...], wk[...]).astype(BF16)
    key_ref[...] = key
    key_t[...] = key.T
    copies[3].wait()
    near[1, WIDTH:, :] = dot(tok[...], wv[...]).astype(BF16).T
    copies[4].start()

    dx_order = (2, 1, 3, 0)

    def send(dx):
        for db in db_order:
            if dx or db:
                rs_copy(dx, db).start()

    def pair_sums(dx):
        pair = (x + dx) & (NX - 1)
        columns = pl.ds(pl.multiple_of(pair * 2 * HEAD_DIM, 2 * HEAD_DIM), 2 * HEAD_DIM)
        logits = dot(key_ref[:, columns], block_diag[pair])
        top = jnp.max(logits, axis=0, keepdims=True)
        weight = jnp.exp(logits - top)
        total = jnp.sum(weight, axis=0, keepdims=True)
        weight = weight.astype(BF16)
        for head in range(2):
            cols = slice(head * SLOTS, (head + 1) * SLOTS)
            start = pl.multiple_of(pair * 2 * HEAD_DIM + head * HEAD_DIM, HEAD_DIM)
            paired = jnp.concatenate(
                [key_t[pl.ds(start, HEAD_DIM), :], near[1, pl.ds(WIDTH + start, HEAD_DIM), :]],
                axis=0,
            )
            sums = dot(paired, weight[:, cols])
            key_sum, value_sum = sums[:HEAD_DIM], sums[HEAD_DIM:]
            key_sum = key_sum - jnp.mean(key_sum, axis=0, keepdims=True)
            stats = stats_block(top[:, cols], total[:, cols]).astype(BF16)
            for quarter, data in enumerate(
                (key_sum[:UNIT], key_sum[UNIT:], value_sum[:UNIT], value_sum[UNIT:])
            ):
                unit = pair * NB + head * 4 + quarter
                units[unit, 0:UNIT, :] = data.astype(BF16)
                units[unit, UNIT:MSG, :] = stats

    pair_sums(2)
    pl.semaphore_wait(barrier, PLANE + NZ - 2)
    send(2)
    pair_sums(1)
    send(1)
    pair_sums(3)
    send(3)
    pair_sums(0)
    send(0)
    for head in range(HEADS):
        rows = slice(head * HEAD_DIM, (head + 1) * HEAD_DIM)
        values = key_t[rows, :].astype(F32)
        center = values - jnp.mean(values, axis=0, keepdims=True)
        spread = jnp.mean(center * center, axis=0, keepdims=True)
        near[1, rows, :] = (center * lax.rsqrt(spread + 1e-05)).astype(BF16)
    pl.when(last)(lambda: relay_copy(0).start())
    pl.when(first)(lambda: relay_copy(1).start())
    copies[4].wait()
    query = dot(tok[...], wq[...]).astype(BF16).astype(F32) * (1.0 / HEAD_DIM**0.5)
    query_t[...] = query.astype(BF16).T

    running = None
    for dx in (0, 1, 3, 2):
        low = 1 if dx == 0 else 0
        group_wait(rs_in.at[pl.ds(dx * NB + low, NB - low), pl.ds(0, MSG)], rs_recv.at[dx])
        parts = [
            (lambda k=k: rs_in[k, UNIT:MSG, :], lambda k=k: rs_in[k, 0:UNIT, :])
            for k in range(dx * NB + low, (dx + 1) * NB)
        ]
        if dx == 0:
            parts.append((lambda: units[me, UNIT:MSG, :], lambda: units[me, 0:UNIT, :]))
        running = merge(parts, running)
    top, total, sums = running
    z_out[0:UNIT, :] = sums.astype(BF16)
    z_out[UNIT:MSG, :] = stats_block(top, total).astype(BF16)
    for dz in dz_order:
        z_copy(dz).start()

    @pl.when(last)
    def _():
        relay_copy(0).wait_recv()
        cross_next.start()

    @pl.when(first)
    def _():
        relay_copy(1).wait_recv()
        cross_prev.start()

    pl.when(jnp.logical_not(last))(halo_next.start)
    pl.when(jnp.logical_not(first))(halo_prev.start)
    group_wait(z_in.at[pl.ds(1, NZ - 1), pl.ds(0, MSG)], z_recv.at[0])
    parts = [
        (lambda k=k: z_in[k, UNIT:MSG, :], lambda k=k: z_in[k, 0:UNIT, :]) for k in range(1, NZ)
    ]
    parts.append((lambda: z_out[UNIT:MSG, :], lambda: z_out[0:UNIT, :]))
    top, total, sums = merge(parts)
    divisor = jnp.where((b & 3) >= 2, total, 1.0)
    slots[me] = (sums / divisor).astype(BF16)
    for dx in (2, 1, 3, 0):
        for db in db_order:
            if dx or db:
                ag_copy(dx, db).start()

    halo_next.wait_recv()
    halo_prev.wait_recv()
    source = lax.broadcasted_iota(jnp.int32, (ROWS, ROWS), 0)
    target = lax.broadcasted_iota(jnp.int32, (ROWS, ROWS), 1)
    line = a * NB + b
    before = (source >= target) & (line > 0)
    after = (source <= target) & (line < DEVICES - 1)
    for head in range(HEADS):
        rows = slice(head * HEAD_DIM, (head + 1) * HEAD_DIM)
        value_rows = slice(WIDTH + head * HEAD_DIM, WIDTH + (head + 1) * HEAD_DIM)
        query_h = query_t[rows, :]
        scores = [
            lax.dot_general(near[i, rows, :], query_h, TN, preferred_element_type=F32)
            for i in range(3)
        ]
        scores[0] = jnp.where(before, scores[0], -1e30)
        scores[2] = jnp.where(after, scores[2], -1e30)
        top_h = jnp.max(
            jnp.maximum(jnp.maximum(scores[0], scores[1]), scores[2]), axis=0, keepdims=True
        )
        exps = [jnp.exp(s - top_h) for s in scores]
        near_top[head] = jnp.broadcast_to(top_h, (8, ROWS))
        near_sum[head] = jnp.broadcast_to(
            jnp.sum(exps[0] + exps[1] + exps[2], axis=0, keepdims=True), (8, ROWS)
        )
        total_h = dot(near[0, value_rows, :], exps[0].astype(BF16))
        total_h = total_h + dot(near[1, value_rows, :], exps[1].astype(BF16))
        acc[rows, :] = total_h + dot(near[2, value_rows, :], exps[2].astype(BF16))

    for dx in (0, 1, 3, 2):
        low = 1 if dx == 0 else 0
        group_wait(slots.at[pl.ds(0, NB - low)], ag_recv.at[dx])
        pair = (x + NX - dx) & (NX - 1)
        results = []
        for half in range(2):
            head = pair * 2 + half
            start = pl.multiple_of(head * HEAD_DIM, HEAD_DIM)
            center = slots[pl.ds(4 * head, 2)].reshape(HEAD_DIM, SLOTS).astype(F32)
            values_h = slots[pl.ds(4 * head + 2, 2)].reshape(HEAD_DIM, SLOTS)
            spread = jnp.mean(center * center, axis=0, keepdims=True)
            keys_h = (center * lax.rsqrt(spread + 1e-05)).astype(BF16)
            scores = lax.dot_general(
                keys_h, query_t[pl.ds(start, HEAD_DIM), :], TN, preferred_element_type=F32
            )
            top_n = near_top[head, 0:1, :]
            top_h = jnp.maximum(top_n, jnp.max(scores, axis=0, keepdims=True))
            exps = jnp.exp(scores - top_h)
            scale = jnp.exp(top_n - top_h)
            denom = scale * near_sum[head, 0:1, :] + jnp.sum(exps, axis=0, keepdims=True)
            result = scale * acc[pl.ds(start, HEAD_DIM), :] + dot(values_h, exps.astype(BF16))
            results.append((result / denom).astype(BF16))
        columns = pl.ds(pl.multiple_of(pair * 2 * HEAD_DIM, 2 * HEAD_DIM), 2 * HEAD_DIM)
        out_ref[:, columns] = jnp.concatenate(results, axis=0).T

    group_wait(rs_in.at[pl.ds(0, PLANE - 1), pl.ds(0, MSG)], rs_send.at[0])
    group_wait(z_in.at[pl.ds(0, NZ - 1), pl.ds(0, MSG)], z_send.at[0])
    group_wait(slots.at[pl.ds(0, PLANE - 1)], ag_send.at[0])
    halo_next.wait_send()
    halo_prev.wait_send()
    pl.when(last | first)(relay_copy(0).wait_send)


def per_device(tokens, w_query, w_key, w_value, w_slot, w_out):
    dma = pltpu.SemaphoreType.DMA
    attended = pl.pallas_call(
        layer,
        out_shape=jax.ShapeDtypeStruct((ROWS, WIDTH), BF16),
        in_specs=[pl.BlockSpec(memory_space=pltpu.HBM)] * 5,
        out_specs=pl.BlockSpec(memory_space=pltpu.VMEM),
        scratch_shapes=[
            pltpu.VMEM((ROWS, D), BF16),
            pltpu.VMEM((D, WIDTH), BF16),
            pltpu.VMEM((D, WIDTH), BF16),
            pltpu.VMEM((D, WIDTH), BF16),
            pltpu.VMEM((HEADS, HEAD_DIM, SLOTS), BF16),
            dma((5,)),
            pltpu.VMEM((HEADS // 2, 2 * HEAD_DIM, 2 * SLOTS), BF16),
            pltpu.VMEM((ROWS, WIDTH), BF16),
            pltpu.VMEM((WIDTH, ROWS), BF16),
            pltpu.VMEM((WIDTH, ROWS), BF16),
            pltpu.VMEM((PLANE, SLOT_ROWS, SLOTS), BF16),
            pltpu.VMEM((PLANE, SLOT_ROWS, SLOTS), BF16),
            pltpu.VMEM((SLOT_ROWS, SLOTS), BF16),
            pltpu.VMEM((NZ, SLOT_ROWS, SLOTS), BF16),
            pltpu.VMEM((PLANE, UNIT, SLOTS), BF16),
            pltpu.VMEM((3, 2 * WIDTH, ROWS), BF16),
            pltpu.VMEM((2 * WIDTH, ROWS), BF16),
            pltpu.VMEM((WIDTH, ROWS), F32),
            pltpu.VMEM((HEADS, 8, ROWS), F32),
            pltpu.VMEM((HEADS, 8, ROWS), F32),
            dma((1,)),
            dma((NX,)),
            dma((1,)),
            dma((1,)),
            dma((1,)),
            dma((NX,)),
            dma((2,)),
            dma((2,)),
            dma((1,)),
            dma((1,)),
        ],
        compiler_params=pltpu.CompilerParams(
            collective_id=0, has_side_effects=True, vmem_limit_bytes=24 * 1024 * 1024
        ),
        name="layer",
    )(*(pltpu.with_memory_space_constraint(v, pltpu.HBM) for v in (tokens, w_query, w_key, w_value, w_slot)))
    return jnp.dot(attended, w_out, preferred_element_type=F32).astype(BF16)


def solution(mesh):
    in_specs = (P(("ctxa", "ctxb"), None), P(), P(), P(), P(), P())
    out_specs = P(("ctxa", "ctxb"), None)
    return jax.shard_map(
        per_device, mesh=mesh, in_specs=in_specs, out_specs=out_specs, check_vma=False
    )
```

```python
import jax
import jax.numpy as jnp
from jax import lax
from jax.experimental import pallas as pl
from jax.experimental.pallas import tpu as pltpu
from jax.sharding import PartitionSpec as P

HEADS = 8
HEAD_DIM = 64
SLOTS = 128
WINDOW = 128
ROWS = 128
D = 1024
WIDTH = HEADS * HEAD_DIM

NX = 4
NZ = 8
NB = 8
NY = 4
PLANE = NX * NB
CHIPS = NX * NY
DEVICES = PLANE * NZ
UNIT = 32
MSG = 40
SLOT_ROWS = 48

BF16 = jnp.bfloat16
F32 = jnp.float32
MESH = pl.DeviceIdType.MESH
TN = (((0,), (0,)), ((), ()))


def dot(a, b):
    return jnp.dot(a, b, preferred_element_type=F32)


def stats_block(top, total):
    row = lax.broadcasted_iota(jnp.int32, (8, SLOTS), 0)
    both = jnp.where(row < 3, top, total)
    high = both.astype(BF16).astype(F32)
    rest = both - high
    mid = rest.astype(BF16).astype(F32)
    low = rest - mid
    part = jnp.where(row < 3, row, row - 3)
    return jnp.where(part == 0, high, jnp.where(part == 1, mid, jnp.where(part == 2, low, 0.0)))


def merge(parts, running=None):
    stats = [load_stats().astype(F32) for load_stats, _ in parts]
    tops = [s[0:1] + s[1:2] + s[2:3] for s in stats]
    totals = [s[3:4] + s[4:5] + s[5:6] for s in stats]
    top = tops[0]
    for other in tops[1:]:
        top = jnp.maximum(top, other)
    if running is None:
        total = jnp.zeros_like(top)
        sums = jnp.zeros((UNIT, SLOTS), F32)
    else:
        old_top, total, sums = running
        top = jnp.maximum(top, old_top)
        scale = jnp.exp(old_top - top)
        total, sums = scale * total, scale * sums
    for k, (_, load_data) in enumerate(parts):
        scale = jnp.exp(tops[k] - top)
        total = total + scale * totals[k]
        sums = sums + scale * load_data().astype(F32)
    return top, total, sums


def layer(
    tok_hbm,
    wq_hbm,
    wk_hbm,
    wv_hbm,
    ws_hbm,
    out_ref,
    tok,
    wq,
    wk,
    wv,
    ws,
    in_sem,
    kv_t,
    other_t,
    query_t,
    units,
    rs_in,
    z_out,
    z_in,
    slots,
    near,
    relay,
    acc,
    near_top,
    near_sum,
    column,
    upward,
    downward,
    swap_send,
    swap_recv,
    rs_send,
    rs_recv,
    z_send,
    z_recv,
    ag_send,
    ag_recv,
    halo_send,
    halo_recv,
    relay_send,
    relay_recv,
):
    a = lax.axis_index("ctxa")
    b = lax.axis_index("ctxb")
    x = a >> 3
    z = a & (NZ - 1)
    y = b >> 1
    c = b & 1
    me = x * NB + c * 4 + y

    pairs = ((ws_hbm, ws), (tok_hbm, tok), (wk_hbm, wk), (wv_hbm, wv), (wq_hbm, wq))
    copies = [
        pltpu.make_async_copy(src, dst, in_sem.at[i]) for i, (src, dst) in enumerate(pairs)
    ]
    for copy in copies[:4]:
        copy.start()

    def device(dx=0, dz=0, db=0):
        return ((((x + dx) & (NX - 1)) << 3) | ((z + dz) & (NZ - 1)), (b + db) & (NB - 1))

    db_order = (4, 3, 5, 2, 6, 1, 7, 0)
    dz_order = (4, 3, 5, 2, 6, 1, 7)
    barrier = pltpu.get_barrier_semaphore()
    greeted = [device(dx=2), device(db=4), (a, b + 1 - 2 * c), device(dz=1), device(dz=NZ - 1)]
    greeted += [device(dx=1), device(dx=3), device(db=2), device(db=6)]
    for other in greeted:
        pl.semaphore_signal(barrier, inc=1, device_id=other, device_id_type=MESH)

    def pass_on(sem, to):
        pl.semaphore_signal(sem, inc=1, device_id=device(dz=to), device_id_type=MESH)

    def wait_greetings():
        pl.semaphore_wait(barrier, len(greeted))
        for dx in (2, 1, 3):
            pl.semaphore_signal(
                column.at[NX - dx], inc=1, device_id=device(dx=dx), device_id_type=MESH
            )
        pass_on(upward.at[0], 1)
        pass_on(downward.at[0], NZ - 1)

    def swap_copy(i):
        return pltpu.make_async_remote_copy(
            src_ref=kv_t.at[i, :, 1 - c],
            dst_ref=other_t.at[i],
            send_sem=swap_send.at[i],
            recv_sem=swap_recv.at[i],
            device_id=(a, b + 1 - 2 * c),
            device_id_type=MESH,
        )

    def rs_copy(dx, dy):
        unit = (((x + dx) & (NX - 1)) << 2) | ((y + dy) & (NY - 1))
        return pltpu.make_async_remote_copy(
            src_ref=units.at[unit, pl.ds(0, MSG)],
            dst_ref=rs_in.at[dx * NY + dy, pl.ds(0, MSG)],
            send_sem=rs_send.at[0],
            recv_sem=rs_recv.at[dx],
            device_id=device(dx=dx, db=2 * dy),
            device_id_type=MESH,
        )

    def z_copy(dz):
        return pltpu.make_async_remote_copy(
            src_ref=z_out.at[pl.ds(0, MSG)],
            dst_ref=z_in.at[dz, pl.ds(0, MSG)],
            send_sem=z_send.at[0],
            recv_sem=z_recv.at[0],
            device_id=device(dz=dz),
            device_id_type=MESH,
        )

    def ag_copy(dx, db):
        return pltpu.make_async_remote_copy(
            src_ref=slots.at[me],
            dst_ref=slots.at[me],
            send_sem=ag_send.at[0],
            recv_sem=ag_recv.at[dx],
            device_id=device(dx=dx, db=db),
            device_id_type=MESH,
        )

    def halo_copy(side, src, target):
        return pltpu.make_async_remote_copy(
            src_ref=src,
            dst_ref=near.at[2 * side],
            send_sem=halo_send.at[side],
            recv_sem=halo_recv.at[side],
            device_id=target,
            device_id_type=MESH,
        )

    def relay_copy(side):
        return pltpu.make_async_remote_copy(
            src_ref=near.at[1],
            dst_ref=relay,
            send_sem=relay_send.at[0],
            recv_sem=relay_recv.at[0],
            device_id=device(dz=1 if side == 0 else NZ - 1),
            device_id_type=MESH,
        )

    last, first = b == NB - 1, b == 0
    halo_next = halo_copy(0, near.at[1], device(db=1))
    halo_prev = halo_copy(1, near.at[1], device(db=NB - 1))
    cross_next = halo_copy(0, relay, device(dx=jnp.where(z == 0, 1, 0), db=1))
    cross_prev = halo_copy(1, relay, device(dx=jnp.where(z == NZ - 1, NX - 1, 0), db=NB - 1))

    def group_wait(ref, sem):
        pltpu.make_async_copy(ref, ref, sem).wait()

    def block_weights(keys_h, slot_map):
        logits = lax.dot_general(keys_h, slot_map, TN, preferred_element_type=F32)
        top = jnp.max(logits, axis=0, keepdims=True)
        weight = jnp.exp(logits - top)
        return top, jnp.sum(weight, axis=0, keepdims=True), weight.astype(BF16)

    copies[1].wait()
    copies[2].wait()
    kv_t[0] = dot(tok[...], wk[...]).astype(BF16).T.reshape(NX, 2, HEAD_DIM, ROWS)
    copies[3].wait()
    value_t = dot(tok[...], wv[...]).astype(BF16).T
    kv_t[1] = value_t.reshape(NX, 2, HEAD_DIM, ROWS)
    wait_greetings()
    swap_copy(0).start()
    swap_copy(1).start()
    copies[4].start()
    near[1, WIDTH:, :] = value_t
    copies[0].wait()
    dx_order = (2, 1, 3, 0)
    heads = [(x + dx) & (NX - 1) for dx in dx_order]
    maps = [ws[2 * p + c] for p in heads]
    own = []
    for p, slot_map in zip(heads, maps):
        top, total, weight = block_weights(kv_t[0, p, c], slot_map)
        paired = jnp.concatenate([kv_t[0, p, c], kv_t[1, p, c]], axis=0)
        own.append((top, total, dot(paired, weight)))
    swap_copy(0).wait_recv()
    swap_copy(1).wait_recv()
    others = [block_weights(other_t[0, p], slot_map) for p, slot_map in zip(heads, maps)]
    for p, (own_top, own_total, own_sums), (top, total, weight) in zip(heads, own, others):
        paired = jnp.concatenate([other_t[0, p], other_t[1, p]], axis=0)
        joint = jnp.maximum(own_top, top)
        own_scale, scale = jnp.exp(own_top - joint), jnp.exp(top - joint)
        sums = own_scale * own_sums + scale * dot(paired, weight)
        key_sum, value_sum = sums[:HEAD_DIM], sums[HEAD_DIM:]
        key_sum = key_sum - jnp.mean(key_sum, axis=0, keepdims=True)
        stats = stats_block(joint, own_scale * own_total + scale * total).astype(BF16)
        for quarter, data in enumerate(
            (key_sum[:UNIT], key_sum[UNIT:], value_sum[:UNIT], value_sum[UNIT:])
        ):
            units[p * NY + quarter, 0:UNIT, :] = data.astype(BF16)
            units[p * NY + quarter, UNIT:MSG, :] = stats
    turn = jnp.where(x == 3, 2, jnp.where(x == 2, 0, x))
    places = [lax.rem(turn + k, 3) for k in (1, 2, 0)]
    for tx in [place + (place >> 1) for place in places] + [2]:
        dx = (tx + NX - x) & (NX - 1)
        pl.when(dx != 0)(lambda dx=dx: pl.semaphore_wait(column.at[dx], 1))
        for dy in (2, 1, 3):
            rs_copy(dx, dy).start()
        pl.when(dx != 0)(rs_copy(dx, 0).start)

    pl.semaphore_wait(upward.at[0], 1)
    pass_on(upward.at[1], 1)
    pl.semaphore_wait(downward.at[0], 1)
    pass_on(downward.at[1], NZ - 1)
    for head in range(HEADS):
        rows = slice(head * HEAD_DIM, (head + 1) * HEAD_DIM)
        values = kv_t[0, head // 2, head % 2].astype(F32)
        center = values - jnp.mean(values, axis=0, keepdims=True)
        spread = jnp.mean(center * center, axis=0, keepdims=True)
        near[1, rows, :] = (center * lax.rsqrt(spread + 1e-05)).astype(BF16)
    pl.when(last)(lambda: relay_copy(0).start())
    pl.when(first)(lambda: relay_copy(1).start())
    pl.semaphore_wait(upward.at[1], 1)
    pass_on(upward.at[2], 1)
    copies[4].wait()
    query = dot(tok[...], wq[...]).astype(BF16).astype(F32) * (1.0 / HEAD_DIM**0.5)
    query_t[...] = query.astype(BF16).T

    pl.semaphore_wait(downward.at[1], 1)
    pl.semaphore_wait(upward.at[2], 1)

    running = None
    for dx in (0, 1, 3, 2):
        low = 1 if dx == 0 else 0
        group_wait(rs_in.at[pl.ds(dx * NY + low, NY - low), pl.ds(0, MSG)], rs_recv.at[dx])
        parts = [
            (lambda k=k: rs_in[k, UNIT:MSG, :], lambda k=k: rs_in[k, 0:UNIT, :])
            for k in range(dx * NY + low, (dx + 1) * NY)
        ]
        if dx == 0:
            mine = x * NY + y
            parts.append((lambda: units[mine, UNIT:MSG, :], lambda: units[mine, 0:UNIT, :]))
        running = merge(parts, running)
    top, total, sums = running
    z_out[0:UNIT, :] = sums.astype(BF16)
    z_out[UNIT:MSG, :] = stats_block(top, total).astype(BF16)
    for dz in dz_order:
        z_copy(dz).start()

    @pl.when(last)
    def _():
        relay_copy(0).wait_recv()
        cross_next.start()

    @pl.when(first)
    def _():
        relay_copy(1).wait_recv()
        cross_prev.start()

    pl.when(jnp.logical_not(last))(halo_next.start)
    pl.when(jnp.logical_not(first))(halo_prev.start)
    group_wait(z_in.at[pl.ds(1, NZ - 1), pl.ds(0, MSG)], z_recv.at[0])
    parts = [
        (lambda k=k: z_in[k, UNIT:MSG, :], lambda k=k: z_in[k, 0:UNIT, :]) for k in range(1, NZ)
    ]
    parts.append((lambda: z_out[UNIT:MSG, :], lambda: z_out[0:UNIT, :]))
    top, total, sums = merge(parts)
    divisor = jnp.where(y >= 2, total, 1.0)
    slots[me] = (sums / divisor).astype(BF16)
    for dx in (2, 1, 3, 0):
        for db in db_order:
            if dx or db:
                ag_copy(dx, db).start()

    halo_next.wait_recv()
    halo_prev.wait_recv()
    source = lax.broadcasted_iota(jnp.int32, (ROWS, ROWS), 0)
    target = lax.broadcasted_iota(jnp.int32, (ROWS, ROWS), 1)
    line = a * NB + b
    before = (source >= target) & (line > 0)
    after = (source <= target) & (line < DEVICES - 1)
    for head in range(HEADS):
        rows = slice(head * HEAD_DIM, (head + 1) * HEAD_DIM)
        value_rows = slice(WIDTH + head * HEAD_DIM, WIDTH + (head + 1) * HEAD_DIM)
        query_h = query_t[rows, :]
        scores = [
            lax.dot_general(near[i, rows, :], query_h, TN, preferred_element_type=F32)
            for i in range(3)
        ]
        scores[0] = jnp.where(before, scores[0], -1e30)
        scores[2] = jnp.where(after, scores[2], -1e30)
        top_h = jnp.max(
            jnp.maximum(jnp.maximum(scores[0], scores[1]), scores[2]), axis=0, keepdims=True
        )
        exps = [jnp.exp(s - top_h) for s in scores]
        near_top[head] = jnp.broadcast_to(top_h, (8, ROWS))
        near_sum[head] = jnp.broadcast_to(
            jnp.sum(exps[0] + exps[1] + exps[2], axis=0, keepdims=True), (8, ROWS)
        )
        total_h = dot(near[0, value_rows, :], exps[0].astype(BF16))
        total_h = total_h + dot(near[1, value_rows, :], exps[1].astype(BF16))
        acc[rows, :] = total_h + dot(near[2, value_rows, :], exps[2].astype(BF16))

    for dx in (0, 1, 3, 2):
        low = 1 if dx == 0 else 0
        group_wait(slots.at[pl.ds(0, NB - low)], ag_recv.at[dx])
        pair = (x + NX - dx) & (NX - 1)
        results = []
        for half in range(2):
            head = pair * 2 + half
            start = pl.multiple_of(head * HEAD_DIM, HEAD_DIM)
            center = slots[pl.ds(4 * head, 2)].reshape(HEAD_DIM, SLOTS).astype(F32)
            values_h = slots[pl.ds(4 * head + 2, 2)].reshape(HEAD_DIM, SLOTS)
            spread = jnp.mean(center * center, axis=0, keepdims=True)
            keys_h = (center * lax.rsqrt(spread + 1e-05)).astype(BF16)
            scores = lax.dot_general(
                keys_h, query_t[pl.ds(start, HEAD_DIM), :], TN, preferred_element_type=F32
            )
            top_n = near_top[head, 0:1, :]
            top_h = jnp.maximum(top_n, jnp.max(scores, axis=0, keepdims=True))
            exps = jnp.exp(scores - top_h)
            scale = jnp.exp(top_n - top_h)
            denom = scale * near_sum[head, 0:1, :] + jnp.sum(exps, axis=0, keepdims=True)
            result = scale * acc[pl.ds(start, HEAD_DIM), :] + dot(values_h, exps.astype(BF16))
            results.append((result / denom).astype(BF16))
        columns = pl.ds(pl.multiple_of(pair * 2 * HEAD_DIM, 2 * HEAD_DIM), 2 * HEAD_DIM)
        out_ref[:, columns] = jnp.concatenate(results, axis=0).T

    group_wait(rs_in.at[pl.ds(0, CHIPS - 1), pl.ds(0, MSG)], rs_send.at[0])
    swap_copy(0).wait_send()
    swap_copy(1).wait_send()
    group_wait(z_in.at[pl.ds(0, NZ - 1), pl.ds(0, MSG)], z_send.at[0])
    group_wait(slots.at[pl.ds(0, PLANE - 1)], ag_send.at[0])
    halo_next.wait_send()
    halo_prev.wait_send()
    pl.when(last | first)(relay_copy(0).wait_send)


def per_device(tokens, w_query, w_key, w_value, w_slot, w_out):
    dma = pltpu.SemaphoreType.DMA
    attended = pl.pallas_call(
        layer,
        out_shape=jax.ShapeDtypeStruct((ROWS, WIDTH), BF16),
        in_specs=[pl.BlockSpec(memory_space=pltpu.HBM)] * 5,
        out_specs=pl.BlockSpec(memory_space=pltpu.VMEM),
        scratch_shapes=[
            pltpu.VMEM((ROWS, D), BF16),
            pltpu.VMEM((D, WIDTH), BF16),
            pltpu.VMEM((D, WIDTH), BF16),
            pltpu.VMEM((D, WIDTH), BF16),
            pltpu.VMEM((HEADS, HEAD_DIM, SLOTS), BF16),
            dma((5,)),
            pltpu.VMEM((2, NX, 2, HEAD_DIM, ROWS), BF16),
            pltpu.VMEM((2, NX, HEAD_DIM, ROWS), BF16),
            pltpu.VMEM((WIDTH, ROWS), BF16),
            pltpu.VMEM((CHIPS, SLOT_ROWS, SLOTS), BF16),
            pltpu.VMEM((CHIPS, SLOT_ROWS, SLOTS), BF16),
            pltpu.VMEM((SLOT_ROWS, SLOTS), BF16),
            pltpu.VMEM((NZ, SLOT_ROWS, SLOTS), BF16),
            pltpu.VMEM((PLANE, UNIT, SLOTS), BF16),
            pltpu.VMEM((3, 2 * WIDTH, ROWS), BF16),
            pltpu.VMEM((2 * WIDTH, ROWS), BF16),
            pltpu.VMEM((WIDTH, ROWS), F32),
            pltpu.VMEM((HEADS, 8, ROWS), F32),
            pltpu.VMEM((HEADS, 8, ROWS), F32),
            pltpu.SemaphoreType.REGULAR((NX,)),
            pltpu.SemaphoreType.REGULAR((3,)),
            pltpu.SemaphoreType.REGULAR((2,)),
            dma((2,)),
            dma((2,)),
            dma((1,)),
            dma((NX,)),
            dma((1,)),
            dma((1,)),
            dma((1,)),
            dma((NX,)),
            dma((2,)),
            dma((2,)),
            dma((1,)),
            dma((1,)),
        ],
        compiler_params=pltpu.CompilerParams(
            collective_id=0, has_side_effects=True, vmem_limit_bytes=24 * 1024 * 1024
        ),
        name="layer",
    )(*(pltpu.with_memory_space_constraint(v, pltpu.HBM) for v in (tokens, w_query, w_key, w_value, w_slot)))
    return jnp.dot(attended, w_out, preferred_element_type=F32).astype(BF16)


def solution(mesh):
    in_specs = (P(("ctxa", "ctxb"), None), P(), P(), P(), P(), P())
    out_specs = P(("ctxa", "ctxb"), None)
    return jax.shard_map(
        per_device, mesh=mesh, in_specs=in_specs, out_specs=out_specs, check_vma=False
    )
```

```python
import jax
import jax.numpy as jnp
from jax import lax
from jax.experimental import pallas as pl
from jax.experimental.pallas import tpu as pltpu
from jax.sharding import PartitionSpec as P

HEADS = 8
HEAD_DIM = 64
SLOTS = 128
WINDOW = 128
ROWS = 128
D = 1024
WIDTH = HEADS * HEAD_DIM

NX = 4
NZ = 8
NB = 8
NY = 4
PLANE = NX * NB
CHIPS = NX * NY
DEVICES = PLANE * NZ
UNIT = 32
MSG = 40
SLOT_ROWS = 48

BF16 = jnp.bfloat16
F32 = jnp.float32
MESH = pl.DeviceIdType.MESH
TN = (((0,), (0,)), ((), ()))


def dot(a, b):
    return jnp.dot(a, b, preferred_element_type=F32)


def stats_block(top, total):
    row = lax.broadcasted_iota(jnp.int32, (8, SLOTS), 0)
    both = jnp.where(row < 3, top, total)
    high = both.astype(BF16).astype(F32)
    rest = both - high
    mid = rest.astype(BF16).astype(F32)
    low = rest - mid
    part = jnp.where(row < 3, row, row - 3)
    return jnp.where(part == 0, high, jnp.where(part == 1, mid, jnp.where(part == 2, low, 0.0)))


def merge(parts, running=None):
    stats = [load_stats().astype(F32) for load_stats, _ in parts]
    tops = [s[0:1] + s[1:2] + s[2:3] for s in stats]
    totals = [s[3:4] + s[4:5] + s[5:6] for s in stats]
    top = tops[0]
    for other in tops[1:]:
        top = jnp.maximum(top, other)
    if running is None:
        total = jnp.zeros_like(top)
        sums = jnp.zeros((UNIT, SLOTS), F32)
    else:
        old_top, total, sums = running
        top = jnp.maximum(top, old_top)
        scale = jnp.exp(old_top - top)
        total, sums = scale * total, scale * sums
    for k, (_, load_data) in enumerate(parts):
        scale = jnp.exp(tops[k] - top)
        total = total + scale * totals[k]
        sums = sums + scale * load_data().astype(F32)
    return top, total, sums


def layer(
    tok_hbm,
    wq_hbm,
    wk_hbm,
    wv_hbm,
    ws_hbm,
    out_ref,
    tok,
    wq,
    wk,
    wv,
    ws,
    in_sem,
    kv_t,
    other_t,
    query_t,
    units,
    rs_in,
    z_out,
    z_in,
    slots,
    near,
    relay,
    acc,
    near_top,
    near_sum,
    column,
    upward,
    downward,
    swap_send,
    swap_recv,
    rs_send,
    rs_recv,
    z_send,
    z_recv,
    ag_send,
    ag_recv,
    halo_send,
    halo_recv,
    relay_send,
    relay_recv,
):
    a = lax.axis_index("ctxa")
    b = lax.axis_index("ctxb")
    x = a >> 3
    z = a & (NZ - 1)
    y = b >> 1
    c = b & 1
    me = x * NB + c * 4 + y

    pairs = ((ws_hbm, ws), (tok_hbm, tok), (wk_hbm, wk), (wv_hbm, wv), (wq_hbm, wq))
    copies = [
        pltpu.make_async_copy(src, dst, in_sem.at[i]) for i, (src, dst) in enumerate(pairs)
    ]
    for copy in copies[:4]:
        copy.start()

    def device(dx=0, dz=0, db=0):
        return ((((x + dx) & (NX - 1)) << 3) | ((z + dz) & (NZ - 1)), (b + db) & (NB - 1))

    db_order = (4, 3, 5, 2, 6, 1, 7, 0)
    dz_order = (4, 3, 5, 2, 6, 1, 7)
    barrier = pltpu.get_barrier_semaphore()
    greeted = [device(dx=2), device(db=4), (a, b + 1 - 2 * c), device(dz=1), device(dz=NZ - 1)]
    greeted += [device(dx=1), device(dx=3), device(db=2), device(db=6)]
    for other in greeted:
        pl.semaphore_signal(barrier, inc=1, device_id=other, device_id_type=MESH)

    def pass_on(sem, to):
        pl.semaphore_signal(sem, inc=1, device_id=device(dz=to), device_id_type=MESH)

    def wait_greetings():
        pl.semaphore_wait(barrier, len(greeted))
        for dx in (2, 1, 3):
            pl.semaphore_signal(
                column.at[NX - dx], inc=1, device_id=device(dx=dx), device_id_type=MESH
            )
        pass_on(upward.at[0], 1)
        pass_on(downward.at[0], NZ - 1)

    def swap_copy(i):
        return pltpu.make_async_remote_copy(
            src_ref=kv_t.at[i, 1 - c],
            dst_ref=other_t.at[i],
            send_sem=swap_send.at[i],
            recv_sem=swap_recv.at[i],
            device_id=(a, b + 1 - 2 * c),
            device_id_type=MESH,
        )

    def rs_copy(dx, dy):
        unit = (((x + dx) & (NX - 1)) << 2) | ((y + dy) & (NY - 1))
        return pltpu.make_async_remote_copy(
            src_ref=units.at[unit, pl.ds(0, MSG)],
            dst_ref=rs_in.at[dx * NY + dy, pl.ds(0, MSG)],
            send_sem=rs_send.at[0],
            recv_sem=rs_recv.at[dx],
            device_id=device(dx=dx, db=2 * dy),
            device_id_type=MESH,
        )

    def z_copy(dz):
        return pltpu.make_async_remote_copy(
            src_ref=z_out.at[pl.ds(0, MSG)],
            dst_ref=z_in.at[dz, pl.ds(0, MSG)],
            send_sem=z_send.at[0],
            recv_sem=z_recv.at[0],
            device_id=device(dz=dz),
            device_id_type=MESH,
        )

    def ag_copy(dx, db):
        return pltpu.make_async_remote_copy(
            src_ref=slots.at[me],
            dst_ref=slots.at[me],
            send_sem=ag_send.at[0],
            recv_sem=ag_recv.at[dx],
            device_id=device(dx=dx, db=db),
            device_id_type=MESH,
        )

    def halo_copy(side, src, target):
        return pltpu.make_async_remote_copy(
            src_ref=src,
            dst_ref=near.at[2 * side],
            send_sem=halo_send.at[side],
            recv_sem=halo_recv.at[side],
            device_id=target,
            device_id_type=MESH,
        )

    def relay_copy(side):
        return pltpu.make_async_remote_copy(
            src_ref=near.at[1],
            dst_ref=relay,
            send_sem=relay_send.at[0],
            recv_sem=relay_recv.at[0],
            device_id=device(dz=1 if side == 0 else NZ - 1),
            device_id_type=MESH,
        )

    last, first = b == NB - 1, b == 0
    halo_next = halo_copy(0, near.at[1], device(db=1))
    halo_prev = halo_copy(1, near.at[1], device(db=NB - 1))
    cross_next = halo_copy(0, relay, device(dx=jnp.where(z == 0, 1, 0), db=1))
    cross_prev = halo_copy(1, relay, device(dx=jnp.where(z == NZ - 1, NX - 1, 0), db=NB - 1))

    def group_wait(ref, sem):
        pltpu.make_async_copy(ref, ref, sem).wait()

    def block_weights(keys_h, slot_map):
        logits = lax.dot_general(keys_h, slot_map, TN, preferred_element_type=F32)
        top = jnp.max(logits, axis=0, keepdims=True)
        weight = jnp.exp(logits - top)
        return top, jnp.sum(weight, axis=0, keepdims=True), weight.astype(BF16)

    copies[1].wait()
    copies[2].wait()
    by_head = dot(tok[...], wk[...]).astype(BF16).T.reshape(NX, 2, HEAD_DIM, ROWS)
    kv_t[0, 0], kv_t[0, 1] = by_head[:, 0], by_head[:, 1]
    copies[3].wait()
    value_t = dot(tok[...], wv[...]).astype(BF16).T
    by_head = value_t.reshape(NX, 2, HEAD_DIM, ROWS)
    kv_t[1, 0], kv_t[1, 1] = by_head[:, 0], by_head[:, 1]
    wait_greetings()
    swap_copy(0).start()
    swap_copy(1).start()
    copies[4].start()
    near[1, WIDTH:, :] = value_t
    copies[0].wait()
    dx_order = (2, 1, 3, 0)
    heads = [(x + dx) & (NX - 1) for dx in dx_order]
    maps = [ws[2 * p + c] for p in heads]
    own = []
    for p, slot_map in zip(heads, maps):
        top, total, weight = block_weights(kv_t[0, c, p], slot_map)
        paired = jnp.concatenate([kv_t[0, c, p], kv_t[1, c, p]], axis=0)
        own.append((top, total, dot(paired, weight)))
    swap_copy(0).wait_recv()
    swap_copy(1).wait_recv()
    others = [block_weights(other_t[0, p], slot_map) for p, slot_map in zip(heads, maps)]
    for p, (own_top, own_total, own_sums), (top, total, weight) in zip(heads, own, others):
        paired = jnp.concatenate([other_t[0, p], other_t[1, p]], axis=0)
        joint = jnp.maximum(own_top, top)
        own_scale, scale = jnp.exp(own_top - joint), jnp.exp(top - joint)
        sums = own_scale * own_sums + scale * dot(paired, weight)
        key_sum, value_sum = sums[:HEAD_DIM], sums[HEAD_DIM:]
        key_sum = key_sum - jnp.mean(key_sum, axis=0, keepdims=True)
        stats = stats_block(joint, own_scale * own_total + scale * total).astype(BF16)
        for quarter, data in enumerate(
            (key_sum[:UNIT], key_sum[UNIT:], value_sum[:UNIT], value_sum[UNIT:])
        ):
            units[p * NY + quarter, 0:UNIT, :] = data.astype(BF16)
            units[p * NY + quarter, UNIT:MSG, :] = stats
    turn = jnp.where(x == 3, 2, jnp.where(x == 2, 0, x))
    places = [lax.rem(turn + k, 3) for k in (1, 2, 0)]
    for tx in [place + (place >> 1) for place in places] + [2]:
        dx = (tx + NX - x) & (NX - 1)
        pl.when(dx != 0)(lambda dx=dx: pl.semaphore_wait(column.at[dx], 1))
        for dy in (2, 1, 3):
            rs_copy(dx, dy).start()
        pl.when(dx != 0)(rs_copy(dx, 0).start)

    pl.semaphore_wait(upward.at[0], 1)
    pass_on(upward.at[1], 1)
    pl.semaphore_wait(downward.at[0], 1)
    pass_on(downward.at[1], NZ - 1)
    for head in range(HEADS):
        rows = slice(head * HEAD_DIM, (head + 1) * HEAD_DIM)
        values = kv_t[0, head % 2, head // 2].astype(F32)
        center = values - jnp.mean(values, axis=0, keepdims=True)
        spread = jnp.mean(center * center, axis=0, keepdims=True)
        near[1, rows, :] = (center * lax.rsqrt(spread + 1e-05)).astype(BF16)
    pl.when(last)(lambda: relay_copy(0).start())
    pl.when(first)(lambda: relay_copy(1).start())
    pl.semaphore_wait(upward.at[1], 1)
    pass_on(upward.at[2], 1)
    copies[4].wait()
    query = dot(tok[...], wq[...]).astype(BF16).astype(F32) * (1.0 / HEAD_DIM**0.5)
    query_t[...] = query.astype(BF16).T

    pl.semaphore_wait(downward.at[1], 1)
    pl.semaphore_wait(upward.at[2], 1)

    running = None
    for dx in (0, 1, 3, 2):
        low = 1 if dx == 0 else 0
        group_wait(rs_in.at[pl.ds(dx * NY + low, NY - low), pl.ds(0, MSG)], rs_recv.at[dx])
        parts = [
            (lambda k=k: rs_in[k, UNIT:MSG, :], lambda k=k: rs_in[k, 0:UNIT, :])
            for k in range(dx * NY + low, (dx + 1) * NY)
        ]
        if dx == 0:
            mine = x * NY + y
            parts.append((lambda: units[mine, UNIT:MSG, :], lambda: units[mine, 0:UNIT, :]))
        running = merge(parts, running)
    top, total, sums = running
    z_out[0:UNIT, :] = sums.astype(BF16)
    z_out[UNIT:MSG, :] = stats_block(top, total).astype(BF16)
    for dz in dz_order:
        z_copy(dz).start()

    @pl.when(last)
    def _():
        relay_copy(0).wait_recv()
        cross_next.start()

    @pl.when(first)
    def _():
        relay_copy(1).wait_recv()
        cross_prev.start()

    pl.when(jnp.logical_not(last))(halo_next.start)
    pl.when(jnp.logical_not(first))(halo_prev.start)
    group_wait(z_in.at[pl.ds(1, NZ - 1), pl.ds(0, MSG)], z_recv.at[0])
    parts = [
        (lambda k=k: z_in[k, UNIT:MSG, :], lambda k=k: z_in[k, 0:UNIT, :]) for k in range(1, NZ)
    ]
    parts.append((lambda: z_out[UNIT:MSG, :], lambda: z_out[0:UNIT, :]))
    top, total, sums = merge(parts)
    divisor = jnp.where(y >= 2, total, 1.0)
    slots[me] = (sums / divisor).astype(BF16)
    for dx in (2, 1, 3, 0):
        for db in db_order:
            if dx or db:
                ag_copy(dx, db).start()

    halo_next.wait_recv()
    halo_prev.wait_recv()
    source = lax.broadcasted_iota(jnp.int32, (ROWS, ROWS), 0)
    target = lax.broadcasted_iota(jnp.int32, (ROWS, ROWS), 1)
    line = a * NB + b
    before = (source >= target) & (line > 0)
    after = (source <= target) & (line < DEVICES - 1)
    for head in range(HEADS):
        rows = slice(head * HEAD_DIM, (head + 1) * HEAD_DIM)
        value_rows = slice(WIDTH + head * HEAD_DIM, WIDTH + (head + 1) * HEAD_DIM)
        query_h = query_t[rows, :]
        scores = [
            lax.dot_general(near[i, rows, :], query_h, TN, preferred_element_type=F32)
            for i in range(3)
        ]
        scores[0] = jnp.where(before, scores[0], -1e30)
        scores[2] = jnp.where(after, scores[2], -1e30)
        top_h = jnp.max(
            jnp.maximum(jnp.maximum(scores[0], scores[1]), scores[2]), axis=0, keepdims=True
        )
        exps = [jnp.exp(s - top_h) for s in scores]
        near_top[head] = jnp.broadcast_to(top_h, (8, ROWS))
        near_sum[head] = jnp.broadcast_to(
            jnp.sum(exps[0] + exps[1] + exps[2], axis=0, keepdims=True), (8, ROWS)
        )
        total_h = dot(near[0, value_rows, :], exps[0].astype(BF16))
        total_h = total_h + dot(near[1, value_rows, :], exps[1].astype(BF16))
        acc[rows, :] = total_h + dot(near[2, value_rows, :], exps[2].astype(BF16))

    for dx in (0, 1, 3, 2):
        low = 1 if dx == 0 else 0
        group_wait(slots.at[pl.ds(0, NB - low)], ag_recv.at[dx])
        pair = (x + NX - dx) & (NX - 1)
        results = []
        for half in range(2):
            head = pair * 2 + half
            start = pl.multiple_of(head * HEAD_DIM, HEAD_DIM)
            center = slots[pl.ds(4 * head, 2)].reshape(HEAD_DIM, SLOTS).astype(F32)
            values_h = slots[pl.ds(4 * head + 2, 2)].reshape(HEAD_DIM, SLOTS)
            spread = jnp.mean(center * center, axis=0, keepdims=True)
            keys_h = (center * lax.rsqrt(spread + 1e-05)).astype(BF16)
            scores = lax.dot_general(
                keys_h, query_t[pl.ds(start, HEAD_DIM), :], TN, preferred_element_type=F32
            )
            top_n = near_top[head, 0:1, :]
            top_h = jnp.maximum(top_n, jnp.max(scores, axis=0, keepdims=True))
            exps = jnp.exp(scores - top_h)
            scale = jnp.exp(top_n - top_h)
            denom = scale * near_sum[head, 0:1, :] + jnp.sum(exps, axis=0, keepdims=True)
            result = scale * acc[pl.ds(start, HEAD_DIM), :] + dot(values_h, exps.astype(BF16))
            results.append((result / denom).astype(BF16))
        columns = pl.ds(pl.multiple_of(pair * 2 * HEAD_DIM, 2 * HEAD_DIM), 2 * HEAD_DIM)
        out_ref[:, columns] = jnp.concatenate(results, axis=0).T

    group_wait(rs_in.at[pl.ds(0, CHIPS - 1), pl.ds(0, MSG)], rs_send.at[0])
    swap_copy(0).wait_send()
    swap_copy(1).wait_send()
    group_wait(z_in.at[pl.ds(0, NZ - 1), pl.ds(0, MSG)], z_send.at[0])
    group_wait(slots.at[pl.ds(0, PLANE - 1)], ag_send.at[0])
    halo_next.wait_send()
    halo_prev.wait_send()
    pl.when(last | first)(relay_copy(0).wait_send)


def per_device(tokens, w_query, w_key, w_value, w_slot, w_out):
    dma = pltpu.SemaphoreType.DMA
    attended = pl.pallas_call(
        layer,
        out_shape=jax.ShapeDtypeStruct((ROWS, WIDTH), BF16),
        in_specs=[pl.BlockSpec(memory_space=pltpu.HBM)] * 5,
        out_specs=pl.BlockSpec(memory_space=pltpu.VMEM),
        scratch_shapes=[
            pltpu.VMEM((ROWS, D), BF16),
            pltpu.VMEM((D, WIDTH), BF16),
            pltpu.VMEM((D, WIDTH), BF16),
            pltpu.VMEM((D, WIDTH), BF16),
            pltpu.VMEM((HEADS, HEAD_DIM, SLOTS), BF16),
            dma((5,)),
            pltpu.VMEM((2, 2, NX, HEAD_DIM, ROWS), BF16),
            pltpu.VMEM((2, NX, HEAD_DIM, ROWS), BF16),
            pltpu.VMEM((WIDTH, ROWS), BF16),
            pltpu.VMEM((CHIPS, SLOT_ROWS, SLOTS), BF16),
            pltpu.VMEM((CHIPS, SLOT_ROWS, SLOTS), BF16),
            pltpu.VMEM((SLOT_ROWS, SLOTS), BF16),
            pltpu.VMEM((NZ, SLOT_ROWS, SLOTS), BF16),
            pltpu.VMEM((PLANE, UNIT, SLOTS), BF16),
            pltpu.VMEM((3, 2 * WIDTH, ROWS), BF16),
            pltpu.VMEM((2 * WIDTH, ROWS), BF16),
            pltpu.VMEM((WIDTH, ROWS), F32),
            pltpu.VMEM((HEADS, 8, ROWS), F32),
            pltpu.VMEM((HEADS, 8, ROWS), F32),
            pltpu.SemaphoreType.REGULAR((NX,)),
            pltpu.SemaphoreType.REGULAR((3,)),
            pltpu.SemaphoreType.REGULAR((2,)),
            dma((2,)),
            dma((2,)),
            dma((1,)),
            dma((NX,)),
            dma((1,)),
            dma((1,)),
            dma((1,)),
            dma((NX,)),
            dma((2,)),
            dma((2,)),
            dma((1,)),
            dma((1,)),
        ],
        compiler_params=pltpu.CompilerParams(
            collective_id=0, has_side_effects=True, vmem_limit_bytes=24 * 1024 * 1024
        ),
        name="layer",
    )(*(pltpu.with_memory_space_constraint(v, pltpu.HBM) for v in (tokens, w_query, w_key, w_value, w_slot)))
    return jnp.dot(attended, w_out, preferred_element_type=F32).astype(BF16)


def solution(mesh):
    in_specs = (P(("ctxa", "ctxb"), None), P(), P(), P(), P(), P())
    out_specs = P(("ctxa", "ctxb"), None)
    return jax.shard_map(
        per_device, mesh=mesh, in_specs=in_specs, out_specs=out_specs, check_vma=False
    )
```

```python
import jax
import jax.numpy as jnp
from jax import lax
from jax.experimental import pallas as pl
from jax.experimental.pallas import tpu as pltpu
from jax.sharding import PartitionSpec as P

HEADS = 8
HEAD_DIM = 64
SLOTS = 128
WINDOW = 128
ROWS = 128
D = 1024
WIDTH = HEADS * HEAD_DIM

NX = 4
NZ = 8
NB = 8
NY = 4
PLANE = NX * NB
CHIPS = NX * NY
DEVICES = PLANE * NZ
UNIT = 32
MSG = 40
SLOT_ROWS = 48

BF16 = jnp.bfloat16
F32 = jnp.float32
MESH = pl.DeviceIdType.MESH
TN = (((0,), (0,)), ((), ()))


def dot(a, b):
    return jnp.dot(a, b, preferred_element_type=F32)


def stats_block(top, total):
    row = lax.broadcasted_iota(jnp.int32, (8, SLOTS), 0)
    both = jnp.where(row < 3, top, total)
    high = both.astype(BF16).astype(F32)
    rest = both - high
    mid = rest.astype(BF16).astype(F32)
    low = rest - mid
    part = jnp.where(row < 3, row, row - 3)
    return jnp.where(part == 0, high, jnp.where(part == 1, mid, jnp.where(part == 2, low, 0.0)))


def merge(parts, running=None):
    stats = [load_stats().astype(F32) for load_stats, _ in parts]
    tops = [s[0:1] + s[1:2] + s[2:3] for s in stats]
    totals = [s[3:4] + s[4:5] + s[5:6] for s in stats]
    top = tops[0]
    for other in tops[1:]:
        top = jnp.maximum(top, other)
    if running is None:
        total = jnp.zeros_like(top)
        sums = jnp.zeros((UNIT, SLOTS), F32)
    else:
        old_top, total, sums = running
        top = jnp.maximum(top, old_top)
        scale = jnp.exp(old_top - top)
        total, sums = scale * total, scale * sums
    for k, (_, load_data) in enumerate(parts):
        scale = jnp.exp(tops[k] - top)
        total = total + scale * totals[k]
        sums = sums + scale * load_data().astype(F32)
    return top, total, sums


def layer(
    tok_hbm,
    wq_hbm,
    wk_hbm,
    wv_hbm,
    ws_hbm,
    out_ref,
    tok,
    wq,
    wk,
    wv,
    ws,
    in_sem,
    kv_t,
    other_t,
    query_t,
    units,
    rs_in,
    z_out,
    z_in,
    slots,
    near,
    relay,
    acc,
    near_top,
    near_sum,
    column,
    upward,
    downward,
    swap_send,
    swap_recv,
    rs_send,
    rs_recv,
    z_send,
    z_recv,
    ag_send,
    ag_recv,
    halo_send,
    halo_recv,
    relay_send,
    relay_recv,
):
    a = lax.axis_index("ctxa")
    b = lax.axis_index("ctxb")
    x = a >> 3
    z = a & (NZ - 1)
    y = b >> 1
    c = b & 1
    me = x * NB + c * 4 + y

    pairs = ((ws_hbm, ws), (tok_hbm, tok), (wk_hbm, wk), (wv_hbm, wv), (wq_hbm, wq))
    copies = [
        pltpu.make_async_copy(src, dst, in_sem.at[i]) for i, (src, dst) in enumerate(pairs)
    ]
    for copy in copies[:4]:
        copy.start()

    def device(dx=0, dz=0, db=0):
        return ((((x + dx) & (NX - 1)) << 3) | ((z + dz) & (NZ - 1)), (b + db) & (NB - 1))

    db_order = (4, 3, 5, 2, 6, 1, 7, 0)
    dz_order = (4, 3, 5, 2, 6, 1, 7)
    barrier = pltpu.get_barrier_semaphore()
    greeted = [device(dx=2), device(db=4), (a, b + 1 - 2 * c), device(dz=1), device(dz=NZ - 1)]
    greeted += [device(dx=1), device(dx=3), device(db=2), device(db=6)]
    for other in greeted:
        pl.semaphore_signal(barrier, inc=1, device_id=other, device_id_type=MESH)

    def pass_on(sem, to):
        pl.semaphore_signal(sem, inc=1, device_id=device(dz=to), device_id_type=MESH)

    def wait_greetings():
        pl.semaphore_wait(barrier, len(greeted))
        for dx in (2, 1, 3):
            pl.semaphore_signal(
                column.at[NX - dx], inc=1, device_id=device(dx=dx), device_id_type=MESH
            )
        pass_on(upward.at[0], 1)
        pass_on(downward.at[0], NZ - 1)

    def swap_copy(i):
        return pltpu.make_async_remote_copy(
            src_ref=kv_t.at[i, 1 - c],
            dst_ref=other_t.at[i],
            send_sem=swap_send.at[i],
            recv_sem=swap_recv.at[i],
            device_id=(a, b + 1 - 2 * c),
            device_id_type=MESH,
        )

    def rs_copy(dx, dy):
        unit = (((x + dx) & (NX - 1)) << 2) | ((y + dy) & (NY - 1))
        return pltpu.make_async_remote_copy(
            src_ref=units.at[unit, pl.ds(0, MSG)],
            dst_ref=rs_in.at[dx * NY + dy, pl.ds(0, MSG)],
            send_sem=rs_send.at[0],
            recv_sem=rs_recv.at[dx],
            device_id=device(dx=dx, db=2 * dy),
            device_id_type=MESH,
        )

    def z_copy(dz):
        return pltpu.make_async_remote_copy(
            src_ref=z_out.at[pl.ds(0, MSG)],
            dst_ref=z_in.at[dz, pl.ds(0, MSG)],
            send_sem=z_send.at[0],
            recv_sem=z_recv.at[0],
            device_id=device(dz=dz),
            device_id_type=MESH,
        )

    def ag_copy(dx, db):
        return pltpu.make_async_remote_copy(
            src_ref=slots.at[me],
            dst_ref=slots.at[me],
            send_sem=ag_send.at[0],
            recv_sem=ag_recv.at[dx],
            device_id=device(dx=dx, db=db),
            device_id_type=MESH,
        )

    def halo_copy(side, src, target):
        return pltpu.make_async_remote_copy(
            src_ref=src,
            dst_ref=near.at[2 * side],
            send_sem=halo_send.at[side],
            recv_sem=halo_recv.at[side],
            device_id=target,
            device_id_type=MESH,
        )

    def relay_copy(side):
        return pltpu.make_async_remote_copy(
            src_ref=near.at[1],
            dst_ref=relay,
            send_sem=relay_send.at[0],
            recv_sem=relay_recv.at[0],
            device_id=device(dz=1 if side == 0 else NZ - 1),
            device_id_type=MESH,
        )

    last, first = b == NB - 1, b == 0
    halo_next = halo_copy(0, near.at[1], device(db=1))
    halo_prev = halo_copy(1, near.at[1], device(db=NB - 1))
    cross_next = halo_copy(0, relay, device(dx=jnp.where(z == 0, 1, 0), db=1))
    cross_prev = halo_copy(1, relay, device(dx=jnp.where(z == NZ - 1, NX - 1, 0), db=NB - 1))

    def group_wait(ref, sem):
        pltpu.make_async_copy(ref, ref, sem).wait()

    def block_weights(keys_h, slot_map):
        logits = lax.dot_general(keys_h, slot_map, TN, preferred_element_type=F32)
        top = jnp.max(logits, axis=0, keepdims=True)
        weight = jnp.exp(logits - top)
        return top, jnp.sum(weight, axis=0, keepdims=True), weight.astype(BF16)

    copies[1].wait()
    copies[2].wait()
    by_head = dot(tok[...], wk[...]).astype(BF16).T.reshape(NX, 2, HEAD_DIM, ROWS)
    kv_t[0, 0], kv_t[0, 1] = by_head[:, 0], by_head[:, 1]
    wait_greetings()
    swap_copy(0).start()
    copies[3].wait()
    value_t = dot(tok[...], wv[...]).astype(BF16).T
    by_head = value_t.reshape(NX, 2, HEAD_DIM, ROWS)
    kv_t[1, 0], kv_t[1, 1] = by_head[:, 0], by_head[:, 1]
    swap_copy(1).start()
    copies[4].start()
    near[1, WIDTH:, :] = value_t
    copies[0].wait()
    dx_order = (2, 1, 3, 0)
    heads = [(x + dx) & (NX - 1) for dx in dx_order]
    maps = [ws[2 * p + c] for p in heads]
    own = []
    for p, slot_map in zip(heads, maps):
        top, total, weight = block_weights(kv_t[0, c, p], slot_map)
        paired = jnp.concatenate([kv_t[0, c, p], kv_t[1, c, p]], axis=0)
        own.append((top, total, dot(paired, weight)))
    swap_copy(0).wait_recv()
    others = [block_weights(other_t[0, p], slot_map) for p, slot_map in zip(heads, maps)]
    swap_copy(1).wait_recv()
    for p, (own_top, own_total, own_sums), (top, total, weight) in zip(heads, own, others):
        paired = jnp.concatenate([other_t[0, p], other_t[1, p]], axis=0)
        joint = jnp.maximum(own_top, top)
        own_scale, scale = jnp.exp(own_top - joint), jnp.exp(top - joint)
        sums = own_scale * own_sums + scale * dot(paired, weight)
        key_sum, value_sum = sums[:HEAD_DIM], sums[HEAD_DIM:]
        key_sum = key_sum - jnp.mean(key_sum, axis=0, keepdims=True)
        stats = stats_block(joint, own_scale * own_total + scale * total).astype(BF16)
        for quarter, data in enumerate(
            (key_sum[:UNIT], key_sum[UNIT:], value_sum[:UNIT], value_sum[UNIT:])
        ):
            units[p * NY + quarter, 0:UNIT, :] = data.astype(BF16)
            units[p * NY + quarter, UNIT:MSG, :] = stats
    turn = jnp.where(x == 3, 2, jnp.where(x == 2, 0, x))
    places = [lax.rem(turn + k, 3) for k in (1, 2, 0)]
    for tx in [place + (place >> 1) for place in places] + [2]:
        dx = (tx + NX - x) & (NX - 1)
        pl.when(dx != 0)(lambda dx=dx: pl.semaphore_wait(column.at[dx], 1))
        for dy in (2, 1, 3):
            rs_copy(dx, dy).start()
        pl.when(dx != 0)(rs_copy(dx, 0).start)

    pl.semaphore_wait(upward.at[0], 1)
    pass_on(upward.at[1], 1)
    pl.semaphore_wait(downward.at[0], 1)
    pass_on(downward.at[1], NZ - 1)
    for head in range(HEADS):
        rows = slice(head * HEAD_DIM, (head + 1) * HEAD_DIM)
        values = kv_t[0, head % 2, head // 2].astype(F32)
        center = values - jnp.mean(values, axis=0, keepdims=True)
        spread = jnp.mean(center * center, axis=0, keepdims=True)
        near[1, rows, :] = (center * lax.rsqrt(spread + 1e-05)).astype(BF16)
    pl.when(last)(lambda: relay_copy(0).start())
    pl.when(first)(lambda: relay_copy(1).start())
    pl.semaphore_wait(upward.at[1], 1)
    pass_on(upward.at[2], 1)
    copies[4].wait()
    query = dot(tok[...], wq[...]).astype(BF16).astype(F32) * (1.0 / HEAD_DIM**0.5)
    query_t[...] = query.astype(BF16).T

    pl.semaphore_wait(downward.at[1], 1)
    pl.semaphore_wait(upward.at[2], 1)

    running = None
    for dx in (0, 1, 3, 2):
        low = 1 if dx == 0 else 0
        group_wait(rs_in.at[pl.ds(dx * NY + low, NY - low), pl.ds(0, MSG)], rs_recv.at[dx])
        parts = [
            (lambda k=k: rs_in[k, UNIT:MSG, :], lambda k=k: rs_in[k, 0:UNIT, :])
            for k in range(dx * NY + low, (dx + 1) * NY)
        ]
        if dx == 0:
            mine = x * NY + y
            parts.append((lambda: units[mine, UNIT:MSG, :], lambda: units[mine, 0:UNIT, :]))
        running = merge(parts, running)
    top, total, sums = running
    z_out[0:UNIT, :] = sums.astype(BF16)
    z_out[UNIT:MSG, :] = stats_block(top, total).astype(BF16)
    for dz in dz_order:
        z_copy(dz).start()

    @pl.when(last)
    def _():
        relay_copy(0).wait_recv()
        cross_next.start()

    @pl.when(first)
    def _():
        relay_copy(1).wait_recv()
        cross_prev.start()

    pl.when(jnp.logical_not(last))(halo_next.start)
    pl.when(jnp.logical_not(first))(halo_prev.start)
    group_wait(z_in.at[pl.ds(1, NZ - 1), pl.ds(0, MSG)], z_recv.at[0])
    parts = [
        (lambda k=k: z_in[k, UNIT:MSG, :], lambda k=k: z_in[k, 0:UNIT, :]) for k in range(1, NZ)
    ]
    parts.append((lambda: z_out[UNIT:MSG, :], lambda: z_out[0:UNIT, :]))
    top, total, sums = merge(parts)
    divisor = jnp.where(y >= 2, total, 1.0)
    slots[me] = (sums / divisor).astype(BF16)
    for dx in (2, 1, 3, 0):
        for db in db_order:
            if dx or db:
                ag_copy(dx, db).start()

    halo_next.wait_recv()
    halo_prev.wait_recv()
    source = lax.broadcasted_iota(jnp.int32, (ROWS, ROWS), 0)
    target = lax.broadcasted_iota(jnp.int32, (ROWS, ROWS), 1)
    line = a * NB + b
    before = (source >= target) & (line > 0)
    after = (source <= target) & (line < DEVICES - 1)
    for head in range(HEADS):
        rows = slice(head * HEAD_DIM, (head + 1) * HEAD_DIM)
        value_rows = slice(WIDTH + head * HEAD_DIM, WIDTH + (head + 1) * HEAD_DIM)
        query_h = query_t[rows, :]
        scores = [
            lax.dot_general(near[i, rows, :], query_h, TN, preferred_element_type=F32)
            for i in range(3)
        ]
        scores[0] = jnp.where(before, scores[0], -1e30)
        scores[2] = jnp.where(after, scores[2], -1e30)
        top_h = jnp.max(
            jnp.maximum(jnp.maximum(scores[0], scores[1]), scores[2]), axis=0, keepdims=True
        )
        exps = [jnp.exp(s - top_h) for s in scores]
        near_top[head] = jnp.broadcast_to(top_h, (8, ROWS))
        near_sum[head] = jnp.broadcast_to(
            jnp.sum(exps[0] + exps[1] + exps[2], axis=0, keepdims=True), (8, ROWS)
        )
        total_h = dot(near[0, value_rows, :], exps[0].astype(BF16))
        total_h = total_h + dot(near[1, value_rows, :], exps[1].astype(BF16))
        acc[rows, :] = total_h + dot(near[2, value_rows, :], exps[2].astype(BF16))

    for dx in (0, 1, 3, 2):
        low = 1 if dx == 0 else 0
        group_wait(slots.at[pl.ds(0, NB - low)], ag_recv.at[dx])
        pair = (x + NX - dx) & (NX - 1)
        results = []
        for half in range(2):
            head = pair * 2 + half
            start = pl.multiple_of(head * HEAD_DIM, HEAD_DIM)
            center = slots[pl.ds(4 * head, 2)].reshape(HEAD_DIM, SLOTS).astype(F32)
            values_h = slots[pl.ds(4 * head + 2, 2)].reshape(HEAD_DIM, SLOTS)
            spread = jnp.mean(center * center, axis=0, keepdims=True)
            keys_h = (center * lax.rsqrt(spread + 1e-05)).astype(BF16)
            scores = lax.dot_general(
                keys_h, query_t[pl.ds(start, HEAD_DIM), :], TN, preferred_element_type=F32
            )
            top_n = near_top[head, 0:1, :]
            top_h = jnp.maximum(top_n, jnp.max(scores, axis=0, keepdims=True))
            exps = jnp.exp(scores - top_h)
            scale = jnp.exp(top_n - top_h)
            denom = scale * near_sum[head, 0:1, :] + jnp.sum(exps, axis=0, keepdims=True)
            result = scale * acc[pl.ds(start, HEAD_DIM), :] + dot(values_h, exps.astype(BF16))
            results.append((result / denom).astype(BF16))
        columns = pl.ds(pl.multiple_of(pair * 2 * HEAD_DIM, 2 * HEAD_DIM), 2 * HEAD_DIM)
        out_ref[:, columns] = jnp.concatenate(results, axis=0).T

    group_wait(rs_in.at[pl.ds(0, CHIPS - 1), pl.ds(0, MSG)], rs_send.at[0])
    swap_copy(0).wait_send()
    swap_copy(1).wait_send()
    group_wait(z_in.at[pl.ds(0, NZ - 1), pl.ds(0, MSG)], z_send.at[0])
    group_wait(slots.at[pl.ds(0, PLANE - 1)], ag_send.at[0])
    halo_next.wait_send()
    halo_prev.wait_send()
    pl.when(last | first)(relay_copy(0).wait_send)


def per_device(tokens, w_query, w_key, w_value, w_slot, w_out):
    dma = pltpu.SemaphoreType.DMA
    attended = pl.pallas_call(
        layer,
        out_shape=jax.ShapeDtypeStruct((ROWS, WIDTH), BF16),
        in_specs=[pl.BlockSpec(memory_space=pltpu.HBM)] * 5,
        out_specs=pl.BlockSpec(memory_space=pltpu.VMEM),
        scratch_shapes=[
            pltpu.VMEM((ROWS, D), BF16),
            pltpu.VMEM((D, WIDTH), BF16),
            pltpu.VMEM((D, WIDTH), BF16),
            pltpu.VMEM((D, WIDTH), BF16),
            pltpu.VMEM((HEADS, HEAD_DIM, SLOTS), BF16),
            dma((5,)),
            pltpu.VMEM((2, 2, NX, HEAD_DIM, ROWS), BF16),
            pltpu.VMEM((2, NX, HEAD_DIM, ROWS), BF16),
            pltpu.VMEM((WIDTH, ROWS), BF16),
            pltpu.VMEM((CHIPS, SLOT_ROWS, SLOTS), BF16),
            pltpu.VMEM((CHIPS, SLOT_ROWS, SLOTS), BF16),
            pltpu.VMEM((SLOT_ROWS, SLOTS), BF16),
            pltpu.VMEM((NZ, SLOT_ROWS, SLOTS), BF16),
            pltpu.VMEM((PLANE, UNIT, SLOTS), BF16),
            pltpu.VMEM((3, 2 * WIDTH, ROWS), BF16),
            pltpu.VMEM((2 * WIDTH, ROWS), BF16),
            pltpu.VMEM((WIDTH, ROWS), F32),
            pltpu.VMEM((HEADS, 8, ROWS), F32),
            pltpu.VMEM((HEADS, 8, ROWS), F32),
            pltpu.SemaphoreType.REGULAR((NX,)),
            pltpu.SemaphoreType.REGULAR((3,)),
            pltpu.SemaphoreType.REGULAR((2,)),
            dma((2,)),
            dma((2,)),
            dma((1,)),
            dma((NX,)),
            dma((1,)),
            dma((1,)),
            dma((1,)),
            dma((NX,)),
            dma((2,)),
            dma((2,)),
            dma((1,)),
            dma((1,)),
        ],
        compiler_params=pltpu.CompilerParams(
            collective_id=0, has_side_effects=True, vmem_limit_bytes=24 * 1024 * 1024
        ),
        name="layer",
    )(*(pltpu.with_memory_space_constraint(v, pltpu.HBM) for v in (tokens, w_query, w_key, w_value, w_slot)))
    return jnp.dot(attended, w_out, preferred_element_type=F32).astype(BF16)


def solution(mesh):
    in_specs = (P(("ctxa", "ctxb"), None), P(), P(), P(), P(), P())
    out_specs = P(("ctxa", "ctxb"), None)
    return jax.shard_map(
        per_device, mesh=mesh, in_specs=in_specs, out_specs=out_specs, check_vma=False
    )
```
